128 devices in a mesh: slab: 64 (over z, y, x), row: 2 (over core).
Axes of the slice: x: 4, y: 4, z: 4, core: 2. Of those that a mesh axis runs over, the one named last changes fastest.
Arguments:
- diag_block: float32 [64, 2, 512, 512], P('slab', None, 'row'), may hold values from -3 to 8
- lower_block: float32 [64, 2, 512, 512], P('slab', None, 'row'), may hold values from -0.4375 to 0.4375
- upper_block: float32 [64, 2, 512, 512], P('slab', None, 'row'), may hold values from -0.4375 to 0.4375
- twist: int32 [64, 512], P('slab'), may hold values from 0 to 511, each once within a row
- excitation: float32 [64, 2, 512, 128], P('slab', None, 'row'), may hold values from -24 to 24
Outputs:
- solution: float32 [64, 2, 512, 128], P('slab', None, 'row')
The draws below stay inside these ranges and needn't reach their ends.
Inputs may be any that keep to these rules, and one draw needn't show every extreme that they name: Each row of twist is a permutation of 0 to 511.
All inputs are finite; a program needn't handle non-finite values.
Results may differ from the reference program's by a relative error of at most 0.00014.
Values sent between devices are 32-bit elements; how exact they have to be, the bound alone decides.
A program may use at most 128 MiB of HBM per device.

```python
import jax
import jax.numpy as jnp
from jax import lax

STRANDS = 512
PATTERNS = 128
NS_STEPS = 3
SLABS = 64


def draw_diag_block(key, part):
    noise_key, resist_key, react_key = jax.random.split(key, 3)
    shape = (SLABS, 2, STRANDS, STRANDS)
    noise = jnp.clip(jax.random.normal(noise_key, shape, jnp.float32), -6.0, 6.0)
    noise = noise * (1.0 / jnp.sqrt(jnp.float32(STRANDS)))
    resist = jax.random.uniform(resist_key, (SLABS, STRANDS), jnp.float32, 4.0, 6.0)
    react = jax.random.uniform(react_key, (SLABS, STRANDS), jnp.float32, -1.0, 1.0)
    identity = (lax.broadcasted_iota(jnp.int32, (STRANDS, STRANDS), 0) == lax.broadcasted_iota(jnp.int32, (STRANDS, STRANDS), 1)).astype(jnp.float32)
    diagonal_part = jnp.stack([resist[:, :, None] * identity, react[:, :, None] * identity], axis=1)
    return noise + diagonal_part


def levels(rng, extent, pieces, low, high):
    factor_of = 1.0
    for position, shards_of in pieces:
        steps = jax.random.uniform(jax.random.fold_in(jax.random.fold_in(rng, 6), position), (shards_of,), jnp.float32, low / len(pieces), high / len(pieces))
        factor_of = factor_of * jnp.repeat(jnp.exp(steps), extent[position] // shards_of).reshape((-1,) + (1,) * (len(extent) - 1 - position))
    return factor_of


def centred(key, dims, deviation, reach, shards=(), held_as=jnp.bfloat16):
    result = deviation * jax.random.normal(key, dims, jnp.float32)
    if shards:
        result = result * levels(key, dims, shards, -0.22, 0.18)
    return jnp.clip(result, -reach, reach).astype(held_as)


def setup_inputs(seed: int = 0) -> dict:
    splits = jax.random.split(jax.random.key(seed), 6)
    diag_block = draw_diag_block(jax.random.fold_in(splits[5], 71), 0)
    lower_block = centred(splits[1], (SLABS, 2, STRANDS, STRANDS), (STRANDS // 3) ** -0.5, 0.4375, ((0, 64), (2, 2)), jnp.float32)
    upper_block = centred(splits[2], (SLABS, 2, STRANDS, STRANDS), (STRANDS // 3) ** -0.5, 0.4375, ((0, 64), (2, 2)), jnp.float32)
    twist = jax.vmap(lambda own: jax.random.permutation(own, STRANDS))(jax.random.split(splits[3], SLABS)).reshape((SLABS, STRANDS)).astype(jnp.int32)
    excitation = centred(splits[4], (SLABS, 2, STRANDS, PATTERNS), 4.0, 24.0, ((0, 64), (2, 2)), jnp.float32)
    return {"diag_block": diag_block, "lower_block": lower_block, "upper_block": upper_block, "twist": twist, "excitation": excitation}


def complex_product(left_mat, right_mat):
    exact = lax.Precision.HIGHEST
    real_part = jnp.matmul(left_mat[..., 0, :, :], right_mat[..., 0, :, :], precision=exact) - jnp.matmul(left_mat[..., 1, :, :], right_mat[..., 1, :, :], precision=exact)
    imag_part = jnp.matmul(left_mat[..., 0, :, :], right_mat[..., 1, :, :], precision=exact) + jnp.matmul(left_mat[..., 1, :, :], right_mat[..., 0, :, :], precision=exact)
    return jnp.stack([real_part, imag_part], axis=-3)


def newton_inverse(blocks):
    identity = jnp.eye(blocks.shape[-1], dtype=blocks.dtype)
    iterate = jnp.stack([0.4 * identity - 0.04 * blocks[:, 0], -0.04 * blocks[:, 1]], axis=1)
    for iteration in range(NS_STEPS - 1):
        iterate = 2.0 * iterate - complex_product(complex_product(iterate, blocks), iterate)
    return iterate


def twist_columns(block, strand_order):
    return jnp.take(block, strand_order, axis=2)


def reference(diag_block, lower_block, upper_block, twist, excitation):
    slab_ids = jnp.arange(SLABS)
    lower_twisted = jax.vmap(twist_columns)(lower_block, twist) * (slab_ids > 0).astype(lower_block.dtype)[:, None, None, None]
    upper_twisted = jax.vmap(twist_columns)(upper_block, twist) * (slab_ids < SLABS - 1).astype(upper_block.dtype)[:, None, None, None]
    lower_odd = lower_twisted[1::2]
    upper_odd = upper_twisted[1::2]
    drive_odd = excitation[1::2]
    first_inverse = newton_inverse(diag_block[1::2])
    from_below = complex_product(lower_twisted[0::2], jnp.roll(first_inverse, 1, axis=0))
    from_above = complex_product(upper_twisted[0::2], first_inverse)
    diag_one = diag_block[0::2] - complex_product(from_below, jnp.roll(upper_odd, 1, axis=0)) - complex_product(from_above, lower_odd)
    lower_one = -complex_product(from_below, jnp.roll(lower_odd, 1, axis=0))
    upper_one = -complex_product(from_above, upper_odd)
    drive_one = excitation[0::2] - complex_product(from_below, jnp.roll(drive_odd, 1, axis=0)) - complex_product(from_above, drive_odd)
    second_inverse = newton_inverse(diag_one[1::2])
    below_two = complex_product(lower_one[0::2], jnp.roll(second_inverse, 1, axis=0))
    above_two = complex_product(upper_one[0::2], second_inverse)
    diag_two = diag_one[0::2] - complex_product(below_two, jnp.roll(upper_one[1::2], 1, axis=0)) - complex_product(above_two, lower_one[1::2])
    drive_two = drive_one[0::2] - complex_product(below_two, jnp.roll(drive_one[1::2], 1, axis=0)) - complex_product(above_two, drive_one[1::2])
    coarse_solution = complex_product(newton_inverse(diag_two), drive_two)
    residual_two = drive_one[1::2] - complex_product(lower_one[1::2], coarse_solution) - complex_product(upper_one[1::2], jnp.roll(coarse_solution, -1, axis=0))
    middle_solution = complex_product(second_inverse, residual_two)
    even_solution = jnp.stack([coarse_solution, middle_solution], axis=1).reshape((SLABS // 2,) + excitation.shape[1:])
    residual_one = drive_odd - complex_product(lower_odd, even_solution) - complex_product(upper_odd, jnp.roll(even_solution, -1, axis=0))
    odd_solution = complex_product(first_inverse, residual_one)
    return jnp.stack([even_solution, odd_solution], axis=1).reshape(excitation.shape)
```

```python
import functools

import jax
import jax.numpy as jnp
from jax import lax
from jax.experimental import pallas as pl
from jax.experimental.pallas import tpu as pltpu
from jax.sharding import PartitionSpec as P

F32 = jnp.float32
BF16 = jnp.bfloat16
N = 512
H = 256
Q = 128

R_A, R_E, R_L, R_U, R_YCI, R_CC, R_CCP = 0, 1, 2, 3, 4, 5, 6
R_D, R_DP = 7, 9
R_ZW, R_YCO = 11, 12
R_YIN = 13
R_YE = 17
R_ZB, R_SA = 19, 20
R_Z = 21
R_SC, R_FIN = 23, 24
N_RECV = 25
N_SEND = 20


def dot(a, b):
    return jnp.dot(a, b, preferred_element_type=F32)


def halves(x):
    high = x.astype(BF16)
    return high, (x - high.astype(F32)).astype(BF16)


def put_split(dst, rs, cs, re, im):
    for plane, value in enumerate((re, im, re + im)):
        high, low = halves(value)
        dst[plane, 0, rs, cs] = high
        dst[plane, 1, rs, cs] = low


def product3(lhs, rs, rhs, cs):
    parts = []
    for plane in range(3):
        ah, al = lhs[plane, 0, rs, :], lhs[plane, 1, rs, :]
        bh, bl = rhs[plane, 0, :, cs], rhs[plane, 1, :, cs]
        parts.append(dot(ah, bh) + dot(ah, bl) + dot(al, bh))
    return parts[0] - parts[1], parts[2] - parts[0] - parts[1]


def product_stack(lhs, rs, stack_high, stack_low):
    real = dot(lhs[0, 0, rs, :], stack_high) + dot(lhs[0, 0, rs, :], stack_low) + dot(lhs[0, 1, rs, :], stack_high)
    imag = dot(lhs[1, 0, rs, :], stack_high) + dot(lhs[1, 0, rs, :], stack_low) + dot(lhs[1, 1, rs, :], stack_high)
    return real[:, :Q] - imag[:, Q:], real[:, Q:] + imag[:, :Q]


def lane_low(shape):
    return lax.broadcasted_iota(jnp.int32, shape, 1) < Q // 2


def vector_product(lhs, stack_ref, emit):
    high, low = halves(stack_ref[...])
    both = jnp.concatenate([high, low], axis=1)
    for t in range(N // H):
        rs = pl.ds(t * H, H)
        out = []
        for plane in range(2):
            wide = dot(lhs[plane, 0, rs, :], both)
            out.append(wide[:, :Q] + wide[:, Q:] + dot(lhs[plane, 1, rs, :], high))
        turned = pltpu.roll(out[1], Q // 2, 1)
        emit(rs, out[0] + jnp.where(lane_low((H, Q)), -turned, turned))


def split_rows(dst, src, row0, scale_identity):
    @pl.loop(0, H // 32)
    def _(t):
        s0 = pl.multiple_of(t * 32, 32)
        d0 = pl.multiple_of(row0 + s0, 32)
        re, im = src[0, pl.ds(s0, 32), :], src[1, pl.ds(s0, 32), :]
        if scale_identity:
            eye = (
                lax.broadcasted_iota(jnp.int32, (32, N), 0) + d0 == lax.broadcasted_iota(jnp.int32, (32, N), 1)
            ).astype(F32)
            re, im = eye - 0.2 * re, -0.2 * im
        put_split(dst, pl.ds(d0, 32), slice(None), re, im)


def split_columns(dst, src, col0, scale_identity):
    c0 = pl.multiple_of(col0, H)

    @pl.loop(0, N // 32)
    def _(t):
        s0 = pl.multiple_of(t * 32, 32)
        re, im = src[0, pl.ds(s0, 32), :], src[1, pl.ds(s0, 32), :]
        if scale_identity:
            eye = (
                lax.broadcasted_iota(jnp.int32, (32, H), 0) + s0 == lax.broadcasted_iota(jnp.int32, (32, H), 1) + c0
            ).astype(F32)
            re, im = eye - 0.2 * re, -0.2 * im
        put_split(dst, pl.ds(s0, 32), pl.ds(c0, H), re, im)


def squares(lhs):
    @pl.loop(0, 2)
    def _(k):
        src, dst = lhs.at[k], lhs.at[k + 1]

        @pl.loop(0, 4)
        def _(t):
            rs = pl.ds(pl.multiple_of((t // 2) * H, H), H)
            cs = pl.ds(pl.multiple_of((t % 2) * H, H), H)
            re, im = product3(src, rs, src, cs)
            put_split(dst, rs, cs, re, im)


def split_x(xs, x):
    @pl.loop(0, N // 32)
    def _(t):
        rs = pl.ds(pl.multiple_of(t * 32, 32), 32)
        put_split(xs, rs, slice(None), x[0, rs, :], x[1, rs, :])


def apply_series(lhs, x, xs):
    split_x(xs.at[0], x)

    @pl.loop(0, 6)
    def _(u):
        k, t = u // 2, u % 2
        rs = pl.ds(pl.multiple_of(t * H, H), H)
        re, im = product3(lhs.at[k], rs, xs.at[k % 2], slice(None))
        re, im = x[0, rs, :] + re, x[1, rs, :] + im
        x[0, rs, :] = re
        x[1, rs, :] = im
        put_split(xs.at[1 - k % 2], rs, slice(None), re, im)


def kernel(
    slabs,
    a_ref, l_ref, u_ref, tw_ref, e_ref, o_ref,
    onehot, lt, ut, a_oth, l_oth, u_oth, x_ci, x_co, x_w, y_oth, cc_own, cc_oth,
    d_own, d_oth, zw_oth, yco_oth, yin, yein, es, e_send, vec, ye, zb, sa, zin, sc, fin,
    lhs, lc, xs, send_sem, recv_sem,
):
    slab = lax.axis_index("slab")
    r = lax.axis_index("row")
    role = lax.rem(slab, 4)
    odd = lax.rem(role, 2) == 1
    plus = lax.rem(slab + 1, slabs)
    minus = lax.rem(slab + slabs - 1, slabs)
    mine, other = r * H, (1 - r) * H
    mine = pl.multiple_of(mine, H)
    other = pl.multiple_of(other, H)
    partner = (slab, 1 - r)

    barrier = pltpu.get_barrier_semaphore()
    for where in (partner, (plus, r), (minus, r)):
        pl.semaphore_signal(barrier, inc=1, device_id=where, device_id_type=pl.DeviceIdType.MESH)
    pl.semaphore_wait(barrier, 3)

    def copy(src, dst, send, recv, where):
        return pltpu.make_async_remote_copy(
            src_ref=src, dst_ref=dst, send_sem=send_sem.at[send], recv_sem=recv_sem.at[recv],
            device_id=where, device_id_type=pl.DeviceIdType.MESH,
        )

    def arrived(dst, recv):
        copy(dst, dst, 0, recv, partner).wait_recv()

    c_a = copy(a_ref, a_oth, 0, R_A, partner)
    c_a.start()

    def stacked(which):
        er, ei = e_ref[0], e_ref[1]
        low = jnp.where(which == 0, er, pltpu.roll(er, Q // 2, 1))
        high = jnp.where(which == 0, pltpu.roll(ei, Q // 2, 1), ei)
        return jnp.where(lane_low((H, Q)), low, high)

    e_send[...] = stacked(1 - r)
    c_e = copy(e_send, es.at[pl.ds(mine, H), :], 1, R_E, partner)
    c_e.start()
    es[pl.ds(mine, H), :] = stacked(r)

    @pl.loop(0, N // 64)
    def _(t):
        s0 = pl.multiple_of(t * 64, 64)
        hit = lax.broadcasted_iota(jnp.int32, (64, N), 0) + s0 == tw_ref[...]
        onehot[pl.ds(s0, 64), :] = hit.astype(F32).astype(BF16)

    keep_l = (slab > 0).astype(F32)
    keep_u = (slab < slabs - 1).astype(F32)
    for src, dst, keep in ((l_ref, lt, keep_l), (u_ref, ut, keep_u)):
        @pl.loop(0, 2)
        def _(t):
            high, low = halves(src[t])
            dst[t] = (dot(high, onehot[...]) + dot(low, onehot[...])) * keep

    def send_columns(x, dst, base_send, base_recv, where):
        out = []
        for j in range(2):
            view = pl.ds(j * Q, Q)
            c = copy(x.at[:, :, view], dst.at[:, :, view], base_send + j, base_recv + j, where)
            c.start()
            out.append(c)
        return out

    @pl.when(odd)
    def _():
        is_b = role == 1
        inner = (jnp.where(is_b, plus, minus), r)
        outer = (jnp.where(is_b, minus, plus), r)
        side = jnp.where(is_b, 0, 1)
        started = []

        def go(c):
            c.start()
            started.append(c)

        @pl.when(jnp.logical_not(is_b))
        def _():
            @pl.loop(0, H // 8)
            def _(t):
                rs = pl.ds(pl.multiple_of(t * 8, 8), 8)
                for plane in range(2):
                    keep = lt[plane, rs, :]
                    lt[plane, rs, :] = ut[plane, rs, :]
                    ut[plane, rs, :] = keep

        go(copy(ut.at[:, :, pl.ds(other, H)], l_oth.at[:, :, pl.ds(0, H)], 2, R_L, partner))
        go(copy(lt.at[:, :, pl.ds(other, H)], u_oth.at[:, :, pl.ds(0, H)], 3, R_U, partner))
        arrived(a_oth, R_A)
        split_rows(lhs.at[0], a_ref, mine, True)
        split_rows(lhs.at[0], a_oth, other, True)
        squares(lhs)

        def gather_x(x, own, oth):
            for plane in range(2):
                x[plane, pl.ds(mine, H), :] = 0.2 * own[plane, :, pl.ds(mine, H)]
                x[plane, pl.ds(other, H), :] = 0.2 * oth[plane, :, pl.ds(0, H)]

        arrived(l_oth.at[:, :, pl.ds(0, H)], R_L)
        gather_x(x_ci, ut, l_oth)
        apply_series(lhs, x_ci, xs)
        started.extend(send_columns(x_ci, yin.at[side], 4, R_YIN + 2 * side, inner))
        go(copy(x_ci, y_oth, 6, R_YCI, partner))

        arrived(es.at[pl.ds(other, H), :], R_E)
        vec[...] = 0.2 * es[...]
        for k in range(3):
            def emit(rs, value, k=k):
                ye[rs, :] = vec[rs, :] + value
            vector_product(lhs.at[k], vec, emit)
            if k < 2:
                vec[...] = ye[...]
        go(copy(ye, yein.at[side], 7, R_YE + side, inner))

        arrived(u_oth.at[:, :, pl.ds(0, H)], R_U)
        gather_x(x_co, lt, u_oth)
        apply_series(lhs, x_co, xs)
        go(copy(x_co, yco_oth, 8, R_YCO, partner))

        arrived(cc_own, R_CC)
        go(copy(cc_own, cc_oth, 9, R_CCP, partner))
        split_rows(lc.at[0], cc_own, mine, False)
        arrived(y_oth, R_YCI)
        split_columns(lc.at[1], x_ci, mine, False)
        split_columns(lc.at[1], y_oth, other, False)
        arrived(cc_oth, R_CCP)
        split_rows(lc.at[0], cc_oth, other, False)

        @pl.loop(0, 2)
        def _(t):
            rs = pl.ds(pl.multiple_of(t * H, H), H)
            re, im = product3(lc.at[0], rs, xs.at[1], slice(None))
            x_w[0, rs, :] = 0.2 * re
            x_w[1, rs, :] = 0.2 * im

        for j in range(2):
            view = pl.ds(j * Q, Q)
            arrived(d_own.at[:, :, view], R_D + j)
            go(copy(d_own.at[:, :, view], d_oth.at[:, :, view], 10 + j, R_DP + j, partner))
        split_columns(lhs.at[0], d_own, mine, True)
        for j in range(2):
            arrived(d_oth.at[:, :, pl.ds(j * Q, Q)], R_DP + j)
        split_columns(lhs.at[0], d_oth, other, True)
        squares(lhs)
        apply_series(lhs, x_w, xs)
        go(copy(x_w, zw_oth, 12, R_ZW, partner))

        @pl.loop(0, 2)
        def _(t):
            rs = pl.ds(pl.multiple_of(t * H, H), H)
            re, im = product3(lc.at[1], rs, xs.at[1], slice(None))
            yin[0, 0, rs, :] = x_co[0, rs, :] + re
            yin[0, 1, rs, :] = x_co[1, rs, :] + im
        started.extend(send_columns(yin.at[0], yin.at[side], 13, R_YIN + 2 * side, outer))

        arrived(yco_oth, R_YCO)
        split_columns(lc.at[2], x_co, mine, False)
        split_columns(lc.at[2], yco_oth, other, False)
        arrived(zw_oth, R_ZW)
        split_columns(lc.at[0], x_w, mine, False)
        split_columns(lc.at[0], zw_oth, other, False)

        arrived(zb, R_ZB)
        def emit_q(rs, value):
            vec[rs, :] = ye[rs, :] - value
        vector_product(lc.at[1], zb, emit_q)
        go(copy(vec, yein.at[side], 15, R_YE + side, outer))

        arrived(sa, R_SA)
        def emit_z(rs, value):
            es[rs, :] = value
        vector_product(lc.at[0], sa, emit_z)
        go(copy(es, zin.at[side], 16, R_Z + side, inner))
        def emit_w(rs, value):
            yein[0, rs, :] = ye[rs, :] - value
        vector_product(lc.at[2], sa, emit_w)

        arrived(sc, R_SC)
        def emit_s(rs, value):
            zin[0, rs, :] = yein[0, rs, :] - value
        vector_product(lc.at[1], sc, emit_s)
        for c in started:
            c.wait_send()

    @pl.when(jnp.logical_not(odd))
    def _():
        is_c = role == 2
        sides = ((jnp.where(is_c, minus, plus), r), (jnp.where(is_c, plus, minus), r))
        started = []

        def go(c):
            c.start()
            started.append(c)

        go(copy(lt, l_oth, 2, R_L, partner))
        go(copy(ut, u_oth, 3, R_U, partner))

        @pl.when(is_c)
        def _():
            copy(lt, cc_own, 4, R_CC, sides[0]).start()
            copy(ut, cc_own, 5, R_CC, sides[1]).start()

        low = jnp.where(is_c, 0, 1)
        split_rows(lc.at[low], lt, mine, False)
        split_rows(lc.at[1 - low], ut, mine, False)
        arrived(l_oth, R_L)
        split_rows(lc.at[low], l_oth, other, False)
        arrived(u_oth, R_U)
        split_rows(lc.at[1 - low], u_oth, other, False)
        arrived(a_oth, R_A)
        arrived(es.at[pl.ds(other, H), :], R_E)

        for j in range(2):
            view = pl.ds(j * Q, Q)
            column = pl.ds(pl.multiple_of(mine + j * Q, Q), Q)
            stacks = []
            for side in range(2):
                arrived(yin.at[side, :, :, view], R_YIN + 2 * side + j)
                stacks.append(halves(jnp.concatenate([yin[side, 0, :, view], yin[side, 1, :, view]], axis=1)))
            for source, row0 in ((a_ref, mine), (a_oth, other)):
                rs = pl.ds(row0, H)
                re, im = source[0, :, column], source[1, :, column]
                for side in range(2):
                    dre, dim = product_stack(lc.at[side], rs, *stacks[side])
                    re, im = re - dre, im - dim
                d_own[0, rs, view] = re
                d_own[1, rs, view] = im
            go(copy(d_own.at[:, :, view], d_oth.at[:, :, view], 6 + j, R_DP + j, partner))

            @pl.when(is_c)
            def _():
                for side in range(2):
                    copy(
                        d_own.at[:, :, view], d_own.at[:, :, view], 8 + 2 * j + side, R_D + j, sides[side]
                    ).start()

        split_columns(lhs.at[0], d_own, mine, True)
        for j in range(2):
            arrived(d_oth.at[:, :, pl.ds(j * Q, Q)], R_DP + j)
        split_columns(lhs.at[0], d_oth, other, True)
        for side in range(2):
            arrived(yein.at[side], R_YE + side)
            def emit_b(rs, value):
                es[rs, :] = es[rs, :] - value
            vector_product(lc.at[side], yein.at[side], emit_b)
        es[...] = 0.2 * es[...]
        zb[...] = es[...]

        @pl.loop(0, 7)
        def _(step):
            def emit_h(rs, value):
                vec[rs, :] = es[rs, :] + value
            vector_product(lhs.at[0], zb, emit_h)
            zb[...] = vec[...]

        @pl.when(is_c)
        def _():
            first = [copy(zb, zb, 12 + side, R_ZB, sides[side]) for side in range(2)]
            for c in first:
                c.start()
            for side in range(2):
                arrived(zin.at[side], R_Z + side)
            sc[...] = zb[...] + zin[0] + zin[1]
            second = [copy(sc, sc, 14 + side, R_SC, sides[side]) for side in range(2)]
            for c in second:
                c.start()
            copy(lt, cc_own, 4, R_CC, sides[0]).wait_send()
            copy(ut, cc_own, 5, R_CC, sides[1]).wait_send()
            for j in range(2):
                view = pl.ds(j * Q, Q)
                for side in range(2):
                    copy(
                        d_own.at[:, :, view], d_own.at[:, :, view], 8 + 2 * j + side, R_D + j, sides[side]
                    ).wait_send()
            for c in first + second:
                c.wait_send()
            zin[0] = sc[...]

        @pl.when(jnp.logical_not(is_c))
        def _():
            both = [copy(zb, sa, 12 + side, R_SA, sides[side]) for side in range(2)]
            for c in both:
                c.start()
            zin[0] = zb[...]
            for c in both:
                c.wait_send()

        for c in started:
            c.wait_send()

    result = zin.at[0]
    c_f = copy(result.at[pl.ds(other, H), :], fin, 17, R_FIN, partner)
    c_f.start()
    own = result[pl.ds(mine, H), :]
    arrived(fin, R_FIN)
    oth = fin[...]
    first = jnp.where(r == 0, own, oth)
    second = jnp.where(r == 0, oth, own)
    low = lane_low((H, Q))
    o_ref[0] = jnp.where(low, first, pltpu.roll(second, Q // 2, 1))
    o_ref[1] = jnp.where(low, pltpu.roll(first, Q // 2, 1), second)
    c_f.wait_send()
    c_a.wait_send()
    c_e.wait_send()


def solution(mesh):
    slabs = mesh.shape["slab"]

    def body(diag_block, lower_block, upper_block, twist, excitation):
        vmem = pl.BlockSpec(memory_space=pltpu.VMEM)
        rows = pltpu.VMEM((2, H, N), F32)
        columns = pltpu.VMEM((2, N, H), F32)
        vector = pltpu.VMEM((N, Q), F32)
        out = pl.pallas_call(
            functools.partial(kernel, slabs),
            out_shape=jax.ShapeDtypeStruct((2, H, Q), F32),
            in_specs=[vmem] * 5,
            out_specs=vmem,
            scratch_shapes=[
                pltpu.VMEM((N, N), BF16),
                rows, rows,
                rows, rows, rows,
                columns, columns, columns, columns,
                rows, rows,
                columns, columns, columns, columns,
                pltpu.VMEM((2, 2, N, H), F32),
                pltpu.VMEM((2, N, Q), F32),
                vector, pltpu.VMEM((H, Q), F32),
                vector, vector, vector, vector,
                pltpu.VMEM((2, N, Q), F32),
                vector, pltpu.VMEM((H, Q), F32),
                pltpu.VMEM((3, 3, 2, N, N), BF16),
                pltpu.VMEM((3, 3, 2, N, N), BF16),
                pltpu.VMEM((2, 3, 2, N, H), BF16),
                pltpu.SemaphoreType.DMA((N_SEND,)),
                pltpu.SemaphoreType.DMA((N_RECV,)),
            ],
            compiler_params=pltpu.CompilerParams(
                collective_id=0, has_side_effects=True, vmem_limit_bytes=60 * 1024 * 1024
            ),
        )(diag_block[0], lower_block[0], upper_block[0], twist, excitation[0])
        return out[None]

    return jax.shard_map(
        body,
        mesh=mesh,
        in_specs=(
            P("slab", None, "row", None),
            P("slab", None, "row", None),
            P("slab", None, "row", None),
            P("slab", None),
            P("slab", None, "row", None),
        ),
        out_specs=P("slab", None, "row", None),
        check_vma=False,
    )
```

```python
import functools

import jax
import jax.numpy as jnp
from jax import lax
from jax.experimental import pallas as pl
from jax.experimental.pallas import tpu as pltpu
from jax.sharding import PartitionSpec as P

F32 = jnp.float32
BF16 = jnp.bfloat16
N = 512
H = 256
Q = 128
C = 4
K = 4

R_A, R_E, R_T, R_CI, R_CO, R_CC, R_CCP, R_FIN, R_ZB = 0, 1, 2, 4, 5, 6, 7, 8, 9
R_YE = 10
R_YCI, R_D, R_DP, R_P, R_R, R_ZWX = 12, 16, 20, 24, 28, 32
R_YIN, R_ZW, R_ZWP, R_S = 36, 44, 52, 60
N_RECV = 68
N_SEND = 64


def dot(a, b):
    return jnp.dot(a, b, preferred_element_type=F32)


def halves(x):
    high = x.astype(BF16)
    return high, (x - high.astype(F32)).astype(BF16)


def put_split(dst, rs, cs, re, im, planes):
    for plane, value in enumerate((re, im, re + im)[:planes]):
        high, low = halves(value)
        dst[plane, 0, rs, cs] = high
        dst[plane, 1, rs, cs] = low


def product3(lhs, rs, rhs, cs):
    parts = []
    for plane in range(3):
        ah, al = lhs[plane, 0, rs, :], lhs[plane, 1, rs, :]
        bh, bl = rhs[plane, 0, :, cs], rhs[plane, 1, :, cs]
        parts.append(dot(ah, bh) + dot(ah, bl) + dot(al, bh))
    return parts[0] - parts[1], parts[2] - parts[0] - parts[1]


def lane_low(shape):
    return lax.broadcasted_iota(jnp.int32, shape, 1) < Q // 2


def turn(x):
    return pltpu.roll(x, Q // 2, 1)


def pack(re, im):
    low = lane_low(re.shape)
    return jnp.where(low, re, turn(im)), jnp.where(low, turn(re), im)


def unpack(first, second):
    low = lane_low(first.shape)
    return jnp.where(low, first, turn(second)), jnp.where(low, turn(first), second)


def vector_product(lhs, stack_ref, emit):
    high, low = halves(stack_ref[...])
    both = jnp.concatenate([high, low], axis=1)
    for t in range(N // H):
        rs = pl.ds(t * H, H)
        out = []
        for plane in range(2):
            wide = dot(lhs[plane, 0, rs, :], both)
            out.append(wide[:, :Q] + wide[:, Q:] + dot(lhs[plane, 1, rs, :], high))
        turned = turn(out[1])
        emit(rs, out[0] + jnp.where(lane_low((H, Q)), -turned, turned))


def put(dst, lhs, src, base=None, scale=1.0):
    def emit(rs, value):
        value = value if scale == 1.0 else scale * value
        dst[rs, :] = value if base is None else base[rs, :] + value

    vector_product(lhs, src, emit)


def identity_minus(re, im, row0, col0):
    eye = (
        lax.broadcasted_iota(jnp.int32, re.shape, 0) + row0 == lax.broadcasted_iota(jnp.int32, re.shape, 1) + col0
    ).astype(F32)
    return eye - 0.2 * re, -0.2 * im


def split_rows(dst, src, row0, inverse, planes):
    @pl.loop(0, H // 32)
    def _(t):
        s0 = pl.multiple_of(t * 32, 32)
        d0 = pl.multiple_of(row0 + s0, 32)
        re, im = src[0, pl.ds(s0, 32), :], src[1, pl.ds(s0, 32), :]
        if inverse:
            re, im = identity_minus(re, im, d0, 0)
        put_split(dst, pl.ds(d0, 32), slice(None), re, im, planes)


def split_chunks(dst, src, col0, inverse, planes):
    @pl.loop(0, N // 32)
    def _(t):
        rs = pl.ds(pl.multiple_of(t * 32, 32), 32)
        for m in range(C // 2):
            c0 = pl.multiple_of(col0 + m * Q, Q)
            re, im = unpack(src[2 * m, rs, :], src[2 * m + 1, rs, :])
            if inverse:
                re, im = identity_minus(re, im, t * 32, c0)
            put_split(dst, rs, pl.ds(c0, Q), re, im, planes)


def stack_rows(dst, dst_row0, src, col0, scale):
    @pl.loop(0, H // 32)
    def _(t):
        rs = pl.ds(pl.multiple_of(t * 32, 32), 32)
        ds = pl.ds(pl.multiple_of(dst_row0 + t * 32, 32), 32)
        for m in range(C // 2):
            cs = pl.ds(pl.multiple_of(col0 + m * Q, Q), Q)
            first, second = pack(src[0, rs, cs], src[1, rs, cs])
            dst[2 * m, ds, :] = scale * first
            dst[2 * m + 1, ds, :] = scale * second


def square(src, dst, planes):
    @pl.loop(0, 4)
    def _(t):
        rs = pl.ds(pl.multiple_of((t // 2) * H, H), H)
        cs = pl.ds(pl.multiple_of((t % 2) * H, H), H)
        re, im = product3(src, rs, src, cs)
        put_split(dst, rs, cs, re, im, planes)


def series(lhs, x, va, vb, fourth):
    put(va, lhs.at[0], x, x)
    put(vb, lhs.at[1], va, va)
    if fourth:
        put(x, lhs.at[2], vb, vb)
    else:
        put(va, lhs.at[1], vb)
        put(x, lhs.at[1], va, vb)


def kernel(
    slabs,
    a_ref, l_ref, u_ref, tw_ref, e_ref, o_ref,
    onehot, tw, a_oth, tw_oth, a_st, st_send, x_ci, x_co, x_w, y_oth, cc_own, cc_oth,
    d_own, d_oth, p_own, p_oth, zwx, r_own, r_oth, yin, zwo, yein, es, e_send,
    va, vb, ye, zb, qv, res, sin, fin, lhs, lc, send_sem, recv_sem,
):
    slab = lax.axis_index("slab")
    r = lax.axis_index("row")
    role = lax.rem(slab, 4)
    odd = lax.rem(role, 2) == 1

    def slab_at(offset):
        return lax.rem(slab + slabs + offset, slabs)

    plus, minus = slab_at(1), slab_at(-1)
    mine = pl.multiple_of(r * H, H)
    other = pl.multiple_of((1 - r) * H, H)
    partner = (slab, 1 - r)

    barrier = pltpu.get_barrier_semaphore()
    for where in (partner, (plus, r), (minus, r), (slab_at(4), r), (slab_at(-4), r)):
        pl.semaphore_signal(barrier, inc=1, device_id=where, device_id_type=pl.DeviceIdType.MESH)
    pl.semaphore_wait(barrier, 5)

    def copy(src, dst, send, recv, where):
        return pltpu.make_async_remote_copy(
            src_ref=src, dst_ref=dst, send_sem=send_sem.at[send], recv_sem=recv_sem.at[recv],
            device_id=where, device_id_type=pl.DeviceIdType.MESH,
        )

    def arrived(dst, recv):
        copy(dst, dst, 0, recv, partner).wait_recv()

    c_a = copy(a_ref, a_oth, 0, R_A, partner)
    c_a.start()

    def stacked(which):
        first, second = pack(e_ref[0], e_ref[1])
        return jnp.where(which == 0, first, second)

    e_send[...] = stacked(1 - r)
    c_e = copy(e_send, es.at[pl.ds(mine, H), :], 1, R_E, partner)
    c_e.start()
    es[pl.ds(mine, H), :] = stacked(r)

    @pl.loop(0, N // 64)
    def _(t):
        s0 = pl.multiple_of(t * 64, 64)
        hit = lax.broadcasted_iota(jnp.int32, (64, N), 0) + s0 == tw_ref[...]
        onehot[pl.ds(s0, 64), :] = hit.astype(F32).astype(BF16)

    place_l = 1 - role // 2
    keep_l = (slab > 0).astype(F32)
    keep_u = (slab < slabs - 1).astype(F32)
    for src, place, keep in ((l_ref, place_l, keep_l), (u_ref, 1 - place_l, keep_u)):
        @pl.loop(0, 2)
        def _(t):
            high, low = halves(src[t])
            tw[place, t] = (dot(high, onehot[...]) + dot(low, onehot[...])) * keep

    def sender(first):
        count = [first]
        pending = []

        def prepare(make, n=1):
            base = count[0]
            count[0] += n
            assert count[0] <= N_SEND
            pending.append((make, base, n))
            return lambda j=0: make(j, base + j).start()

        def finish():
            for make, base, n in pending:
                for j in range(n):
                    make(j, base + j).wait_send()

        return prepare, finish

    @pl.when(odd)
    def _():
        is_b = role == 1
        inner = (jnp.where(is_b, plus, minus), r)
        outer = (jnp.where(is_b, minus, plus), r)
        sibling = (jnp.where(is_b, slab_at(-4), slab_at(4)), r)
        side = jnp.where(is_b, 0, 1)
        prepare, finish = sender(2)

        s_ci = prepare(lambda j, s: copy(st_send.at[0], x_ci.at[:, pl.ds(mine, H), :], s, R_CI, partner))
        s_co = prepare(lambda j, s: copy(st_send.at[1], x_co.at[:, pl.ds(mine, H), :], s, R_CO, partner))
        s_yci = prepare(lambda j, s: copy(x_ci.at[j], yin.at[side, j], s, R_YIN + 4 * side + j, inner), C)
        s_ycip = prepare(lambda j, s: copy(x_ci.at[j], y_oth.at[j], s, R_YCI + j, partner), C)
        s_ye = prepare(lambda j, s: copy(ye, yein.at[side], s, R_YE + side, inner))
        s_cc = prepare(lambda j, s: copy(cc_own, cc_oth, s, R_CCP, partner))
        s_d = prepare(lambda j, s: copy(d_own.at[j], d_oth.at[j], s, R_DP + j, partner), C)
        s_p = prepare(lambda j, s: copy(p_own.at[j], yin.at[side, j], s, R_YIN + 4 * side + j, outer), C)
        s_pp = prepare(lambda j, s: copy(p_own.at[j], p_oth.at[j], s, R_P + j, partner), C)
        s_zw = prepare(lambda j, s: copy(x_w.at[j], yin.at[side, j], s, R_ZW + 4 * side + j, inner), C)
        s_q = prepare(lambda j, s: copy(qv, yein.at[side], s, R_YE + side, outer))
        s_r = prepare(lambda j, s: copy(r_own.at[j], r_oth.at[j], s, R_R + j, partner), C)

        def piece(ref, j):
            return ref.at[pl.ds(j * Q, Q), :]

        s_in = prepare(lambda j, s: copy(piece(sin.at[0], j), piece(sin.at[side], j), s, R_S + 4 * side + j, inner), K)
        s_sib = prepare(lambda j, s: copy(piece(sin.at[0], j), piece(sin.at[1], j), s, R_S + 4 + j, sibling), K)

        stack_rows(st_send.at[0], 0, tw.at[0], other, 0.2)
        s_ci()
        stack_rows(x_ci, mine, tw.at[0], mine, 0.2)
        arrived(a_oth, R_A)
        split_rows(lhs.at[0], a_ref, mine, True, 3)
        split_rows(lhs.at[0], a_oth, other, True, 3)
        square(lhs.at[0], lhs.at[1], 3)
        arrived(x_ci.at[:, pl.ds(other, H), :], R_CI)
        series(lhs, x_ci.at[0], va, vb, False)
        s_yci(0)
        s_ycip(0)
        square(lhs.at[1], lhs.at[2], 2)

        @pl.loop(1, C)
        def _(j):
            series(lhs, x_ci.at[j], va, vb, True)
            s_yci(j)
            s_ycip(j)

        stack_rows(st_send.at[1], 0, tw.at[1], other, 0.2)
        s_co()
        stack_rows(x_co, mine, tw.at[1], mine, 0.2)
        arrived(es.at[pl.ds(other, H), :], R_E)
        ye[...] = 0.2 * es[...]
        series(lhs, ye, va, vb, True)
        s_ye()
        arrived(x_co.at[:, pl.ds(other, H), :], R_CO)

        @pl.loop(0, C)
        def _(j):
            series(lhs, x_co.at[j], va, vb, True)

        arrived(cc_own, R_CC)
        s_cc()
        split_rows(lc.at[0], cc_own, mine, False, 2)
        split_chunks(lc.at[1], x_ci, mine, False, 2)
        for j in range(C):
            arrived(y_oth.at[j], R_YCI + j)
        split_chunks(lc.at[1], y_oth, other, False, 2)
        arrived(cc_oth, R_CCP)
        split_rows(lc.at[0], cc_oth, other, False, 2)

        @pl.loop(0, C)
        def _(j):
            put(x_w.at[j], lc.at[0], x_co.at[j], scale=0.2)

        for j in range(C):
            arrived(d_own.at[j], R_D + j)
            s_d(j)
        split_chunks(lhs.at[0], d_own, mine, True, 3)
        for j in range(C):
            arrived(d_oth.at[j], R_DP + j)
        split_chunks(lhs.at[0], d_oth, other, True, 3)
        square(lhs.at[0], lhs.at[1], 3)

        def reduced(j, fourth):
            series(lhs, x_w.at[j], va, vb, fourth)
            s_zw(j)
            put(p_own.at[j], lc.at[1], x_w.at[j], x_co.at[j])
            s_p(j)
            s_pp(j)

        reduced(0, False)
        square(lhs.at[1], lhs.at[2], 2)

        @pl.loop(1, C)
        def _(j):
            reduced(j, True)

        arrived(zb, R_ZB)
        put(qv, lc.at[1], zb, ye, -1.0)
        s_q()
        split_chunks(lc.at[2], p_own, mine, False, 2)
        for j in range(C):
            arrived(p_oth.at[j], R_P + j)
        split_chunks(lc.at[2], p_oth, other, False, 2)

        @pl.loop(0, C)
        def _(j):
            arrived(zwx.at[j], R_ZWX + j)
            put(r_own.at[j], lc.at[1], zwx.at[j])
            s_r(j)

        split_chunks(lc.at[0], r_own, mine, False, 2)
        for j in range(C):
            arrived(r_oth.at[j], R_R + j)
        split_chunks(lc.at[0], r_oth, other, False, 2)

        for j in range(K):
            arrived(piece(sin.at[0], j), R_S + j)
            s_in(j)
            s_sib(j)
        put(va, lc.at[2], sin.at[0], qv, -1.0)
        for j in range(K):
            arrived(piece(sin.at[1], j), R_S + 4 + j)
        put(res, lc.at[0], sin.at[1], va, -1.0)
        finish()

    @pl.when(jnp.logical_not(odd))
    def _():
        is_c = role == 2
        sides = ((jnp.where(is_c, minus, plus), r), (jnp.where(is_c, plus, minus), r))
        prepare, finish = sender(2)
        prepare_c, finish_c = sender(24)
        prepare_a, finish_a = sender(24)

        def piece(ref, j):
            return ref.at[pl.ds(j * Q, Q), :]

        s_t = prepare(lambda j, s: copy(tw.at[j], tw_oth.at[j], s, R_T + j, partner), 2)
        s_d = prepare(lambda j, s: copy(d_own.at[j], d_oth.at[j], s, R_DP + j, partner), C)
        s_cc = [prepare_c(lambda j, s, i=i: copy(tw.at[i], cc_own, s, R_CC, sides[i])) for i in range(2)]
        s_dc = [prepare_c(lambda j, s, i=i: copy(d_own.at[j], d_own.at[j], s, R_D + j, sides[i]), C) for i in range(2)]
        s_zb = [prepare_c(lambda j, s, i=i: copy(zb, zb, s, R_ZB, sides[i])) for i in range(2)]
        s_zwp = [
            prepare_c(lambda j, s, i=i: copy(yin.at[i, j], zwo.at[i, j], s, R_ZWP + 4 * i + j, partner), C)
            for i in range(2)
        ]
        s_zwx = [
            prepare_c(lambda j, s, i=i: copy(yin.at[i, j], zwx.at[j], s, R_ZWX + j, sides[1 - i]), C) for i in range(2)
        ]
        s_sa = [
            prepare_a(lambda j, s, i=i: copy(piece(zb, j), piece(sin.at[0], j), s, R_S + j, sides[i]), K)
            for i in range(2)
        ]

        for i in range(2):
            s_t(i)

            @pl.when(is_c)
            def _():
                s_cc[i]()

            split_rows(lc.at[i], tw.at[i], mine, False, 2)
        stack_rows(a_st, mine, a_ref, mine, 1.0)
        arrived(a_oth, R_A)
        stack_rows(a_st, other, a_oth, mine, 1.0)
        for i in range(2):
            arrived(tw_oth.at[i], R_T + i)
            split_rows(lc.at[i], tw_oth.at[i], other, False, 2)
        arrived(es.at[pl.ds(other, H), :], R_E)

        @pl.loop(0, C)
        def _(j):
            arrived(yin.at[0, j], R_YIN + j)
            put(d_own.at[j], lc.at[0], yin.at[0, j], a_st.at[j], -1.0)
            arrived(yin.at[1, j], R_YIN + 4 + j)
            put(d_own.at[j], lc.at[1], yin.at[1, j], d_own.at[j], -1.0)

            @pl.when(is_c)
            def _():
                for i in range(2):
                    s_dc[i](j)

            s_d(j)

        split_chunks(lhs.at[0], d_own, mine, True, 3)
        for j in range(C):
            arrived(d_oth.at[j], R_DP + j)
        split_chunks(lhs.at[0], d_oth, other, True, 3)
        square(lhs.at[0], lhs.at[1], 2)
        for i in range(2):
            arrived(yein.at[i], R_YE + i)
            put(es, lc.at[i], yein.at[i], es, -1.0)
        zb[...] = 0.2 * es[...]
        series(lhs, zb, va, vb, False)

        @pl.when(is_c)
        def _():
            for i in range(2):
                s_zb[i]()

            @pl.loop(0, C)
            def _(j):
                for i in range(2):
                    arrived(yin.at[i, j], R_ZW + 4 * i + j)
                    s_zwx[i](j)
                    s_zwp[i](j)

            for i in range(2):
                split_chunks(lc.at[i], yin.at[i], mine, False, 2)
            for i in range(2):
                for j in range(C):
                    arrived(zwo.at[i, j], R_ZWP + 4 * i + j)
                split_chunks(lc.at[i], zwo.at[i], other, False, 2)
            for i in range(2):
                for j in range(K):
                    arrived(piece(sin.at[i], j), R_S + 4 * i + j)
                put(res, lc.at[i], sin.at[i], zb if i == 0 else res)
            finish_c()

        @pl.when(jnp.logical_not(is_c))
        def _():
            for j in range(K):
                for i in range(2):
                    s_sa[i](j)
            res[...] = zb[...]
            finish_a()

        finish()

    c_f = copy(res.at[pl.ds(other, H), :], fin, N_SEND, R_FIN, partner)
    c_f.start()
    own = res[pl.ds(mine, H), :]
    arrived(fin, R_FIN)
    oth = fin[...]
    re, im = unpack(jnp.where(r == 0, own, oth), jnp.where(r == 0, oth, own))
    o_ref[0] = re
    o_ref[1] = im
    c_f.wait_send()
    c_a.wait_send()
    c_e.wait_send()


def solution(mesh):
    slabs = mesh.shape["slab"]

    def body(diag_block, lower_block, upper_block, twist, excitation):
        vmem = pl.BlockSpec(memory_space=pltpu.VMEM)

        def f32(*shape):
            return pltpu.VMEM(shape, F32)

        rows, chunks, vector = f32(2, H, N), f32(C, N, Q), f32(N, Q)
        out = pl.pallas_call(
            functools.partial(kernel, slabs),
            out_shape=jax.ShapeDtypeStruct((2, H, Q), F32),
            in_specs=[vmem] * 5,
            out_specs=vmem,
            scratch_shapes=[
                pltpu.VMEM((N, N), BF16),
                f32(2, 2, H, N), rows, f32(2, 2, H, N),
                chunks, f32(2, C, H, Q),
                chunks, chunks, chunks, chunks,
                rows, rows,
                chunks, chunks, chunks, chunks,
                chunks, chunks, chunks,
                f32(2, C, N, Q), f32(2, C, N, Q), f32(2, N, Q),
                vector, f32(H, Q),
                vector, vector, vector, vector, vector, vector,
                f32(2, N, Q), f32(H, Q),
                pltpu.VMEM((3, 3, 2, N, N), BF16),
                pltpu.VMEM((3, 2, 2, N, N), BF16),
                pltpu.SemaphoreType.DMA((N_SEND + 1,)),
                pltpu.SemaphoreType.DMA((N_RECV,)),
            ],
            compiler_params=pltpu.CompilerParams(
                collective_id=0, has_side_effects=True, vmem_limit_bytes=60 * 1024 * 1024
            ),
        )(diag_block[0], lower_block[0], upper_block[0], twist, excitation[0])
        return out[None]

    spec = P("slab", None, "row", None)
    return jax.shard_map(
        body,
        mesh=mesh,
        in_specs=(spec, spec, spec, P("slab", None), spec),
        out_specs=spec,
        check_vma=False,
    )
```

```python
import functools

import jax
import jax.numpy as jnp
from jax import lax
from jax.experimental import pallas as pl
from jax.experimental.pallas import tpu as pltpu
from jax.sharding import PartitionSpec as P

F32 = jnp.float32
BF16 = jnp.bfloat16
N = 512
H = 256
Q = 128
C = 4
K = 4

R_A, R_E, R_T, R_CI, R_CO, R_CC, R_CCP, R_FIN, R_ZB = 0, 1, 2, 4, 5, 6, 7, 8, 9
R_YE = 10
R_YCI, R_D, R_DP, R_P, R_R, R_ZWX = 12, 16, 20, 24, 28, 32
R_YIN, R_ZW, R_ZWP, R_S = 36, 44, 52, 60
R_CT = 68
N_RECV = 69
N_SEND = 64


def dot(a, b):
    return jnp.dot(a, b, preferred_element_type=F32)


def halves(x):
    high = x.astype(BF16)
    return high, (x - high.astype(F32)).astype(BF16)


def put_split(dst, rs, cs, re, im, planes):
    for plane, value in enumerate((re, im, re + im)[:planes]):
        high, low = halves(value)
        dst[plane, 0, rs, cs] = high
        dst[plane, 1, rs, cs] = low


def product3(lhs, rs, rhs, cs):
    parts = []
    for plane in range(3):
        ah, al = lhs[plane, 0, rs, :], lhs[plane, 1, rs, :]
        bh, bl = rhs[plane, 0, :, cs], rhs[plane, 1, :, cs]
        parts.append(dot(ah, bh) + dot(ah, bl) + dot(al, bh))
    return parts[0] - parts[1], parts[2] - parts[0] - parts[1]


def lane_low(shape):
    return lax.broadcasted_iota(jnp.int32, shape, 1) < Q // 2


def turn(x):
    return pltpu.roll(x, Q // 2, 1)


def pack(re, im):
    low = lane_low(re.shape)
    return jnp.where(low, re, turn(im)), jnp.where(low, turn(re), im)


def unpack(first, second):
    low = lane_low(first.shape)
    return jnp.where(low, first, turn(second)), jnp.where(low, turn(first), second)


def vector_product(lhs, stack_ref, emit):
    high, low = halves(stack_ref[...])
    both = jnp.concatenate([high, low], axis=1)
    for t in range(N // H):
        rs = pl.ds(t * H, H)
        out = []
        for plane in range(2):
            wide = dot(lhs[plane, 0, rs, :], both)
            out.append(wide[:, :Q] + wide[:, Q:] + dot(lhs[plane, 1, rs, :], high))
        turned = turn(out[1])
        emit(rs, out[0] + jnp.where(lane_low((H, Q)), -turned, turned))


def put(dst, lhs, src, base=None, scale=1.0):
    def emit(rs, value):
        value = value if scale == 1.0 else scale * value
        dst[rs, :] = value if base is None else base[rs, :] + value

    vector_product(lhs, src, emit)


def identity_minus(re, im, row0, col0):
    eye = (
        lax.broadcasted_iota(jnp.int32, re.shape, 0) + row0 == lax.broadcasted_iota(jnp.int32, re.shape, 1) + col0
    ).astype(F32)
    return eye - 0.2 * re, -0.2 * im


def split_rows(dst, src, row0, inverse, planes):
    @pl.loop(0, H // 32)
    def _(t):
        s0 = pl.multiple_of(t * 32, 32)
        d0 = pl.multiple_of(row0 + s0, 32)
        re, im = src[0, pl.ds(s0, 32), :], src[1, pl.ds(s0, 32), :]
        if inverse:
            re, im = identity_minus(re, im, d0, 0)
        put_split(dst, pl.ds(d0, 32), slice(None), re, im, planes)


def split_chunks(dst, src, col0, inverse, planes):
    @pl.loop(0, N // 32)
    def _(t):
        rs = pl.ds(pl.multiple_of(t * 32, 32), 32)
        for m in range(C // 2):
            c0 = pl.multiple_of(col0 + m * Q, Q)
            re, im = unpack(src[2 * m, rs, :], src[2 * m + 1, rs, :])
            if inverse:
                re, im = identity_minus(re, im, t * 32, c0)
            put_split(dst, rs, pl.ds(c0, Q), re, im, planes)


def stack_rows(dst, dst_row0, src, col0, scale):
    @pl.loop(0, H // 32)
    def _(t):
        rs = pl.ds(pl.multiple_of(t * 32, 32), 32)
        ds = pl.ds(pl.multiple_of(dst_row0 + t * 32, 32), 32)
        for m in range(C // 2):
            cs = pl.ds(pl.multiple_of(col0 + m * Q, Q), Q)
            first, second = pack(src[0, rs, cs], src[1, rs, cs])
            dst[2 * m, ds, :] = scale * first
            dst[2 * m + 1, ds, :] = scale * second


def square(src, dst, planes):
    @pl.loop(0, 4)
    def _(t):
        rs = pl.ds(pl.multiple_of((t // 2) * H, H), H)
        cs = pl.ds(pl.multiple_of((t % 2) * H, H), H)
        re, im = product3(src, rs, src, cs)
        put_split(dst, rs, cs, re, im, planes)


def series(lhs, x, va, vb, fourth):
    put(va, lhs.at[0], x, x)
    put(vb, lhs.at[1], va, va)
    if fourth:
        put(x, lhs.at[2], vb, vb)
    else:
        put(va, lhs.at[1], vb)
        put(x, lhs.at[1], va, vb)


def kernel(
    slabs,
    a_ref, l_ref, u_ref, tw_ref, e_ref, o_ref,
    a_own, l_own, u_own, e_own, t_own, t_oth, onehot, tw, a_oth, tw_oth, a_st, st_send, x_ci, x_co, x_w, y_oth, cc_own, cc_oth,
    d_own, d_oth, p_own, p_oth, zwx, r_own, r_oth, yin, zwo, yein, es, e_send,
    va, vb, ye, zb, qv, res, sin, fin, lhs, lc, send_sem, recv_sem, load_sem,
):
    slab = lax.axis_index("slab")
    r = lax.axis_index("row")
    role = lax.rem(slab, 4)
    odd = lax.rem(role, 2) == 1

    loads = []
    for k, (src, dst) in enumerate(((a_ref, a_own), (tw_ref, t_own), (l_ref, l_own), (u_ref, u_own), (e_ref, e_own))):
        load = pltpu.make_async_copy(src, dst, load_sem.at[k])
        load.start()
        loads.append(load)

    def slab_at(offset):
        return lax.rem(slab + slabs + offset, slabs)

    plus, minus = slab_at(1), slab_at(-1)
    has_plus, has_minus = slab < slabs - 1, slab > 0
    mine = pl.multiple_of(r * H, H)
    other = pl.multiple_of((1 - r) * H, H)
    partner = (slab, 1 - r)

    barrier = pltpu.get_barrier_semaphore()
    everyone = (
        (slab >= 0, partner),
        (has_plus, (plus, r)),
        (has_minus, (minus, r)),
        (jnp.logical_and(odd, slab >= 4), (slab_at(-4), r)),
        (jnp.logical_and(odd, slab < slabs - 4), (slab_at(4), r)),
        (slab == 0, (slab_at(3), r)),
        (slab == 3, (slab_at(-3), r)),
    )
    total = 0
    for there, where in everyone:
        @pl.when(there)
        def _():
            pl.semaphore_signal(barrier, inc=1, device_id=where, device_id_type=pl.DeviceIdType.MESH)

        total = total + there.astype(jnp.int32)
    pl.semaphore_wait(barrier, total)

    def copy(src, dst, send, recv, where):
        return pltpu.make_async_remote_copy(
            src_ref=src, dst_ref=dst, send_sem=send_sem.at[send], recv_sem=recv_sem.at[recv],
            device_id=where, device_id_type=pl.DeviceIdType.MESH,
        )

    def arrived(dst, recv):
        copy(dst, dst, 0, recv, partner).wait_recv()

    c_a = copy(a_ref, a_oth, 0, R_A, partner)
    c_a.start()
    couplings = []
    for i, (src, where) in enumerate(((l_ref, (minus, r)), (u_ref, (plus, r)))):
        couplings.append(copy(tw_ref, t_oth, N_SEND + 1 + 2 * i, R_CT, where))
        couplings.append(copy(src, cc_own, N_SEND + 2 + 2 * i, R_CC, where))

    @pl.when(role == 2)
    def _():
        for c in couplings:
            c.start()

    for load in loads:
        load.wait()

    def stacked(which):
        first, second = pack(e_own[0], e_own[1])
        return jnp.where(which == 0, first, second)

    e_send[...] = stacked(1 - r)
    c_e = copy(e_send, es.at[pl.ds(mine, H), :], 1, R_E, partner)
    c_e.start()
    es[pl.ds(mine, H), :] = stacked(r)

    def choose(order):
        @pl.loop(0, N // 64)
        def _(t):
            s0 = pl.multiple_of(t * 64, 64)
            hit = lax.broadcasted_iota(jnp.int32, (64, N), 0) + s0 == order[...]
            onehot[pl.ds(s0, 64), :] = hit.astype(F32).astype(BF16)

    choose(t_own)

    place_l = 1 - role // 2
    keep_l = (slab > 0).astype(F32)
    keep_u = (slab < slabs - 1).astype(F32)
    for src, place, keep in ((l_own, place_l, keep_l), (u_own, 1 - place_l, keep_u)):
        @pl.loop(0, 2)
        def _(t):
            high, low = halves(src[t])
            tw[place, t] = (dot(high, onehot[...]) + dot(low, onehot[...])) * keep

    def twist_rows(dst, src, row0):
        rs = pl.ds(row0, H)

        @pl.loop(0, 2)
        def _(t):
            for part, value in enumerate(halves(src[t])):
                dst[t, part, rs, :] = dot(value, onehot[...]).astype(BF16)

    def sender(first):
        count = [first]
        pending = []

        def prepare(make, n=1, when=None):
            base = count[0]
            count[0] += n
            assert count[0] <= N_SEND
            pending.append((make, base, n, when))

            def start(j=0):
                if when is None:
                    make(j, base + j).start()
                else:
                    pl.when(when)(lambda: make(j, base + j).start())

            return start

        def finish():
            for make, base, n, when in pending:
                def wait(make=make, base=base, n=n):
                    for j in range(n):
                        make(j, base + j).wait_send()

                if when is None:
                    wait()
                else:
                    pl.when(when)(wait)

        return prepare, finish

    @pl.when(odd)
    def _():
        is_b = role == 1
        inner = (jnp.where(is_b, plus, minus), r)
        outer = (jnp.where(is_b, minus, plus), r)
        sibling = (jnp.where(is_b, slab_at(-4), slab_at(4)), r)
        has_outer = has_plus
        has_sibling = jnp.where(is_b, slab >= 4, slab < slabs - 4)
        has_second = jnp.logical_or(jnp.logical_not(is_b), slab < slabs - 4)
        side = jnp.where(is_b, 0, 1)
        prepare, finish = sender(2)

        s_ci = prepare(lambda j, s: copy(st_send.at[0], x_ci.at[:, pl.ds(mine, H), :], s, R_CI, partner))
        s_co = prepare(lambda j, s: copy(st_send.at[1], x_co.at[:, pl.ds(mine, H), :], s, R_CO, partner))
        s_yci = prepare(lambda j, s: copy(x_ci.at[j], yin.at[side, j], s, R_YIN + 4 * side + j, inner), C)
        s_ycip = prepare(lambda j, s: copy(x_ci.at[j], y_oth.at[j], s, R_YCI + j, partner), C)
        s_ye = prepare(lambda j, s: copy(ye, yein.at[side], s, R_YE + side, inner))
        s_cc = prepare(lambda j, s: copy(cc_own, cc_oth, s, R_CCP, partner))
        s_d = prepare(lambda j, s: copy(d_own.at[j], d_oth.at[j], s, R_DP + j, partner), C)
        s_p = prepare(lambda j, s: copy(p_own.at[j], yin.at[side, j], s, R_YIN + 4 * side + j, outer), C, has_outer)
        s_pp = prepare(lambda j, s: copy(p_own.at[j], p_oth.at[j], s, R_P + j, partner), C)
        s_zw = prepare(lambda j, s: copy(x_w.at[j], yin.at[side, j], s, R_ZW + 4 * side + j, inner), C)
        s_q = prepare(lambda j, s: copy(qv, yein.at[side], s, R_YE + side, outer), 1, has_outer)
        s_r = prepare(lambda j, s: copy(r_own.at[j], r_oth.at[j], s, R_R + j, partner), C)

        def piece(ref, j):
            return ref.at[pl.ds(j * Q, Q), :]

        s_in = prepare(lambda j, s: copy(piece(sin.at[0], j), piece(sin.at[side], j), s, R_S + 4 * side + j, inner), K, has_outer)
        s_sib = prepare(lambda j, s: copy(piece(sin.at[0], j), piece(sin.at[1], j), s, R_S + 4 + j, sibling), K, has_sibling)

        stack_rows(st_send.at[0], 0, tw.at[0], other, 0.2)
        s_ci()
        stack_rows(x_ci, mine, tw.at[0], mine, 0.2)
        arrived(a_oth, R_A)
        split_rows(lhs.at[0], a_own, mine, True, 3)
        split_rows(lhs.at[0], a_oth, other, True, 3)
        square(lhs.at[0], lhs.at[1], 3)
        arrived(x_ci.at[:, pl.ds(other, H), :], R_CI)
        series(lhs, x_ci.at[0], va, vb, False)
        s_yci(0)
        s_ycip(0)
        square(lhs.at[1], lhs.at[2], 2)

        @pl.loop(1, C)
        def _(j):
            series(lhs, x_ci.at[j], va, vb, True)
            s_yci(j)
            s_ycip(j)

        stack_rows(st_send.at[1], 0, tw.at[1], other, 0.2)
        s_co()
        stack_rows(x_co, mine, tw.at[1], mine, 0.2)
        arrived(es.at[pl.ds(other, H), :], R_E)
        ye[...] = 0.2 * es[...]
        series(lhs, ye, va, vb, True)
        s_ye()
        arrived(x_co.at[:, pl.ds(other, H), :], R_CO)

        @pl.loop(0, C)
        def _(j):
            series(lhs, x_co.at[j], va, vb, True)

        arrived(t_oth, R_CT)
        choose(t_oth)
        arrived(cc_own, R_CC)
        s_cc()
        twist_rows(lc.at[0], cc_own, mine)
        split_chunks(lc.at[1], x_ci, mine, False, 2)
        for j in range(C):
            arrived(y_oth.at[j], R_YCI + j)
        split_chunks(lc.at[1], y_oth, other, False, 2)
        arrived(cc_oth, R_CCP)
        twist_rows(lc.at[0], cc_oth, other)

        @pl.loop(0, C)
        def _(j):
            put(x_w.at[j], lc.at[0], x_co.at[j], scale=0.2)

        for j in range(C):
            arrived(d_own.at[j], R_D + j)
            s_d(j)
        split_chunks(lhs.at[0], d_own, mine, True, 3)
        for j in range(C):
            arrived(d_oth.at[j], R_DP + j)
        split_chunks(lhs.at[0], d_oth, other, True, 3)
        square(lhs.at[0], lhs.at[1], 3)

        def reduced(j, fourth):
            series(lhs, x_w.at[j], va, vb, fourth)
            s_zw(j)
            put(p_own.at[j], lc.at[1], x_w.at[j], x_co.at[j])
            s_p(j)
            s_pp(j)

        reduced(0, False)
        square(lhs.at[1], lhs.at[2], 2)

        @pl.loop(1, C)
        def _(j):
            reduced(j, True)

        arrived(zb, R_ZB)
        put(qv, lc.at[1], zb, ye, -1.0)
        s_q()
        split_chunks(lc.at[2], p_own, mine, False, 2)
        for j in range(C):
            arrived(p_oth.at[j], R_P + j)
        split_chunks(lc.at[2], p_oth, other, False, 2)

        @pl.loop(0, C)
        def _(j):
            arrived(zwx.at[j], R_ZWX + j)
            put(r_own.at[j], lc.at[1], zwx.at[j])
            s_r(j)

        split_chunks(lc.at[0], r_own, mine, False, 2)
        for j in range(C):
            arrived(r_oth.at[j], R_R + j)
        split_chunks(lc.at[0], r_oth, other, False, 2)

        res[...] = qv[...]

        @pl.when(has_outer)
        def _():
            for j in range(K):
                arrived(piece(sin.at[0], j), R_S + j)
                s_in(j)
                s_sib(j)
            put(res, lc.at[2], sin.at[0], res, -1.0)

        @pl.when(has_second)
        def _():
            for j in range(K):
                arrived(piece(sin.at[1], j), R_S + 4 + j)
            put(res, lc.at[0], sin.at[1], res, -1.0)

        finish()

    @pl.when(jnp.logical_not(odd))
    def _():
        is_c = role == 2
        sides = ((jnp.where(is_c, minus, plus), r), (jnp.where(is_c, plus, minus), r))
        prepare, finish = sender(2)
        prepare_c, finish_c = sender(24)
        prepare_a, finish_a = sender(24)

        def piece(ref, j):
            return ref.at[pl.ds(j * Q, Q), :]

        s_t = prepare(lambda j, s: copy(tw.at[j], tw_oth.at[j], s, R_T + j, partner), 2)
        s_d = prepare(lambda j, s: copy(d_own.at[j], d_oth.at[j], s, R_DP + j, partner), C)
        s_dc = [prepare_c(lambda j, s, i=i: copy(d_own.at[j], d_own.at[j], s, R_D + j, sides[i]), C) for i in range(2)]
        s_zb = [prepare_c(lambda j, s, i=i: copy(zb, zb, s, R_ZB, sides[i])) for i in range(2)]
        s_zwp = [
            prepare_c(lambda j, s, i=i: copy(yin.at[i, j], zwo.at[i, j], s, R_ZWP + 4 * i + j, partner), C)
            for i in range(2)
        ]
        s_zwx = [
            prepare_c(lambda j, s, i=i: copy(yin.at[i, j], zwx.at[j], s, R_ZWX + j, sides[1 - i]), C) for i in range(2)
        ]
        place = jnp.where(slab == 0, 1, 0)
        below = (jnp.where(slab == 0, slab_at(3), minus), r)
        s_sa = [
            prepare_a(lambda j, s: copy(piece(zb, j), piece(sin.at[0], j), s, R_S + j, sides[0]), K),
            prepare_a(lambda j, s: copy(piece(zb, j), piece(sin.at[place], j), s, R_S + 4 * place + j, below), K),
        ]

        for i in range(2):
            s_t(i)
            split_rows(lc.at[i], tw.at[i], mine, False, 2)
        stack_rows(a_st, mine, a_own, mine, 1.0)
        arrived(a_oth, R_A)
        stack_rows(a_st, other, a_oth, mine, 1.0)
        for i in range(2):
            arrived(tw_oth.at[i], R_T + i)
            split_rows(lc.at[i], tw_oth.at[i], other, False, 2)
        arrived(es.at[pl.ds(other, H), :], R_E)

        @pl.loop(0, C)
        def _(j):
            arrived(yin.at[0, j], R_YIN + j)
            put(d_own.at[j], lc.at[0], yin.at[0, j], a_st.at[j], -1.0)

            @pl.when(has_minus)
            def _():
                arrived(yin.at[1, j], R_YIN + 4 + j)
                put(d_own.at[j], lc.at[1], yin.at[1, j], d_own.at[j], -1.0)

            @pl.when(is_c)
            def _():
                for i in range(2):
                    s_dc[i](j)

            s_d(j)

        split_chunks(lhs.at[0], d_own, mine, True, 3)
        for j in range(C):
            arrived(d_oth.at[j], R_DP + j)
        split_chunks(lhs.at[0], d_oth, other, True, 3)
        square(lhs.at[0], lhs.at[1], 2)
        for i in range(2):
            @pl.when(slab >= i)
            def _():
                arrived(yein.at[i], R_YE + i)
                put(es, lc.at[i], yein.at[i], es, -1.0)

        zb[...] = 0.2 * es[...]
        series(lhs, zb, va, vb, False)

        @pl.when(is_c)
        def _():
            for i in range(2):
                s_zb[i]()

            @pl.loop(0, C)
            def _(j):
                for i in range(2):
                    arrived(yin.at[i, j], R_ZW + 4 * i + j)
                    s_zwx[i](j)
                    s_zwp[i](j)

            for i in range(2):
                split_chunks(lc.at[i], yin.at[i], mine, False, 2)
            for i in range(2):
                for j in range(C):
                    arrived(zwo.at[i, j], R_ZWP + 4 * i + j)
                split_chunks(lc.at[i], zwo.at[i], other, False, 2)
            res[...] = zb[...]
            for i in range(2):
                @pl.when(slab < slabs - 1 - i)
                def _():
                    for j in range(K):
                        arrived(piece(sin.at[i], j), R_S + 4 * i + j)
                    put(res, lc.at[i], sin.at[i], res)

            finish_c()
            for c in couplings:
                c.wait_send()

        @pl.when(jnp.logical_not(is_c))
        def _():
            for j in range(K):
                for i in range(2):
                    s_sa[i](j)
            res[...] = zb[...]
            finish_a()

        finish()

    c_f = copy(res.at[pl.ds(other, H), :], fin, N_SEND, R_FIN, partner)
    c_f.start()
    own = res[pl.ds(mine, H), :]
    arrived(fin, R_FIN)
    oth = fin[...]
    re, im = unpack(jnp.where(r == 0, own, oth), jnp.where(r == 0, oth, own))
    o_ref[0] = re
    o_ref[1] = im
    c_f.wait_send()
    c_a.wait_send()
    c_e.wait_send()


def solution(mesh):
    slabs = mesh.shape["slab"]

    def body(diag_block, lower_block, upper_block, twist, excitation):
        vmem = pl.BlockSpec(memory_space=pltpu.VMEM)

        def f32(*shape):
            return pltpu.VMEM(shape, F32)

        rows, chunks, vector = f32(2, H, N), f32(C, N, Q), f32(N, Q)
        out = pl.pallas_call(
            functools.partial(kernel, slabs),
            out_shape=jax.ShapeDtypeStruct((2, H, Q), F32),
            in_specs=[pl.BlockSpec(memory_space=pl.ANY)] * 5,
            out_specs=vmem,
            scratch_shapes=[
                rows, rows, rows, f32(2, H, Q),
                pltpu.VMEM((1, N), jnp.int32), pltpu.VMEM((1, N), jnp.int32),
                pltpu.VMEM((N, N), BF16),
                f32(2, 2, H, N), rows, f32(2, 2, H, N),
                chunks, f32(2, C, H, Q),
                chunks, chunks, chunks, chunks,
                rows, rows,
                chunks, chunks, chunks, chunks,
                chunks, chunks, chunks,
                f32(2, C, N, Q), f32(2, C, N, Q), f32(2, N, Q),
                vector, f32(H, Q),
                vector, vector, vector, vector, vector, vector,
                f32(2, N, Q), f32(H, Q),
                pltpu.VMEM((3, 3, 2, N, N), BF16),
                pltpu.VMEM((3, 2, 2, N, N), BF16),
                pltpu.SemaphoreType.DMA((N_SEND + 5,)),
                pltpu.SemaphoreType.DMA((N_RECV,)),
                pltpu.SemaphoreType.DMA((5,)),
            ],
            compiler_params=pltpu.CompilerParams(
                collective_id=0, has_side_effects=True, vmem_limit_bytes=60 * 1024 * 1024
            ),
        )(diag_block[0], lower_block[0], upper_block[0], twist, excitation[0])
        return out[None]

    spec = P("slab", None, "row", None)
    return jax.shard_map(
        body,
        mesh=mesh,
        in_specs=(spec, spec, spec, P("slab", None), spec),
        out_specs=spec,
        check_vma=False,
    )
```

```python
import functools

import jax
import jax.numpy as jnp
from jax import lax
from jax.experimental import pallas as pl
from jax.experimental.pallas import tpu as pltpu
from jax.sharding import PartitionSpec as P

F32 = jnp.float32
BF16 = jnp.bfloat16
N = 512
H = 256
Q = 128
C = 4
K = 4

R_A, R_E, R_T, R_CI, R_CO, R_FIN, R_ZB = 0, 1, 2, 4, 5, 8, 9
R_YE = 10
R_YCI, R_D, R_DP, R_P, R_R, R_ZWX = 12, 16, 20, 24, 28, 32
R_YIN, R_ZWP, R_S = 36, 52, 60
R_W, R_YCO = 76, 80
N_RECV = 88
N_SEND = 72


def dot(a, b):
    return jnp.dot(a, b, preferred_element_type=F32)


def halves(x):
    high = x.astype(BF16)
    return high, (x - high.astype(F32)).astype(BF16)


def put_split(dst, rs, cs, re, im, planes):
    for plane, value in enumerate((re, im, re + im)[:planes]):
        high, low = halves(value)
        dst[plane, 0, rs, cs] = high
        dst[plane, 1, rs, cs] = low


def product3(lhs, rs, rhs, cs):
    parts = []
    for plane in range(3):
        ah, al = lhs[plane, 0, rs, :], lhs[plane, 1, rs, :]
        bh, bl = rhs[plane, 0, :, cs], rhs[plane, 1, :, cs]
        parts.append(dot(ah, bh) + dot(ah, bl) + dot(al, bh))
    return parts[0] - parts[1], parts[2] - parts[0] - parts[1]


def lane_low(shape):
    return lax.broadcasted_iota(jnp.int32, shape, 1) < Q // 2


def turn(x):
    return pltpu.roll(x, Q // 2, 1)


def pack(re, im):
    low = lane_low(re.shape)
    return jnp.where(low, re, turn(im)), jnp.where(low, turn(re), im)


def unpack(first, second):
    low = lane_low(first.shape)
    return jnp.where(low, first, turn(second)), jnp.where(low, turn(first), second)


def vector_product(lhs, stack_ref, emit):
    high, low = halves(stack_ref[...])
    both = jnp.concatenate([high, low], axis=1)
    for t in range(N // H):
        rs = pl.ds(t * H, H)
        out = []
        for plane in range(2):
            wide = dot(lhs[plane, 0, rs, :], both)
            out.append(wide[:, :Q] + wide[:, Q:] + dot(lhs[plane, 1, rs, :], high))
        turned = turn(out[1])
        emit(t, out[0] + jnp.where(lane_low((H, Q)), -turned, turned))


def put(dst, lhs, src, base=None, scale=1.0, ready=None):
    def emit(t, value):
        rs = pl.ds(t * H, H)
        value = value if scale == 1.0 else scale * value
        dst[rs, :] = value if base is None else base[rs, :] + value
        if ready is not None:
            ready(t)

    vector_product(lhs, src, emit)


def identity_minus(re, im, row0, col0):
    eye = (
        lax.broadcasted_iota(jnp.int32, re.shape, 0) + row0 == lax.broadcasted_iota(jnp.int32, re.shape, 1) + col0
    ).astype(F32)
    return eye - 0.2 * re, -0.2 * im


def split_rows(dst, src, row0, inverse, planes):
    @pl.loop(0, H // 32)
    def _(t):
        s0 = pl.multiple_of(t * 32, 32)
        d0 = pl.multiple_of(row0 + s0, 32)
        re, im = src[0, pl.ds(s0, 32), :], src[1, pl.ds(s0, 32), :]
        if inverse:
            re, im = identity_minus(re, im, d0, 0)
        put_split(dst, pl.ds(d0, 32), slice(None), re, im, planes)


def split_chunks(dst, src, col0, inverse, planes):
    @pl.loop(0, N // 32)
    def _(t):
        rs = pl.ds(pl.multiple_of(t * 32, 32), 32)
        for m in range(C // 2):
            c0 = pl.multiple_of(col0 + m * Q, Q)
            re, im = unpack(src[2 * m, rs, :], src[2 * m + 1, rs, :])
            if inverse:
                re, im = identity_minus(re, im, t * 32, c0)
            put_split(dst, rs, pl.ds(c0, Q), re, im, planes)


def stack_rows(dst, dst_row0, src, col0, scale):
    @pl.loop(0, H // 32)
    def _(t):
        rs = pl.ds(pl.multiple_of(t * 32, 32), 32)
        ds = pl.ds(pl.multiple_of(dst_row0 + t * 32, 32), 32)
        for m in range(C // 2):
            cs = pl.ds(pl.multiple_of(col0 + m * Q, Q), Q)
            first, second = pack(src[0, rs, cs], src[1, rs, cs])
            dst[2 * m, ds, :] = scale * first
            dst[2 * m + 1, ds, :] = scale * second


def square(src, dst):
    @pl.loop(0, 4)
    def _(t):
        rs = pl.ds(pl.multiple_of((t // 2) * H, H), H)
        cs = pl.ds(pl.multiple_of((t % 2) * H, H), H)
        re, im = product3(src, rs, src, cs)
        put_split(dst, rs, cs, re, im, 2)


def series(lhs, src, dst, va, vb, ready=None):
    put(va, lhs.at[0], src, src)
    put(vb, lhs.at[1], va, va)
    put(va, lhs.at[1], vb)
    put(dst, lhs.at[1], va, vb, ready=ready)


def kernel(
    slabs,
    a_ref, l_ref, u_ref, tw_ref, e_ref, o_ref,
    a_own, lu_own, e_own, t_own, onehot, tw, a_oth, tw_oth, a_st, st_send, x_ci, x_co, x_w, y_oth, wco,
    d_own, d_oth, p_own, p_oth, zwx, r_own, r_oth, yin, zwo, yein, es, e_send,
    va, vb, ye, zb, qv, res, sin, fin, lhs, lc, send_sem, recv_sem, load_sem,
):
    slab = lax.axis_index("slab")
    r = lax.axis_index("row")
    role = lax.rem(slab, 4)
    odd = lax.rem(role, 2) == 1

    loads = []
    for k, (src, dst) in enumerate(((a_ref, a_own), (tw_ref, t_own), (l_ref, lu_own.at[0]), (u_ref, lu_own.at[1]), (e_ref, e_own))):
        load = pltpu.make_async_copy(src, dst, load_sem.at[k])
        load.start()
        loads.append(load)

    def slab_at(offset):
        return lax.rem(slab + slabs + offset, slabs)

    plus, minus = slab_at(1), slab_at(-1)
    has_plus, has_minus = slab < slabs - 1, slab > 0
    mine = pl.multiple_of(r * H, H)
    other = pl.multiple_of((1 - r) * H, H)
    partner = (slab, 1 - r)

    barrier = pltpu.get_barrier_semaphore()
    everyone = (
        (slab >= 0, partner),
        (has_plus, (plus, r)),
        (has_minus, (minus, r)),
        (jnp.logical_and(odd, slab >= 4), (slab_at(-4), r)),
        (jnp.logical_and(odd, slab < slabs - 4), (slab_at(4), r)),
        (slab == 0, (slab_at(3), r)),
        (slab == 3, (slab_at(-3), r)),
    )
    total = 0
    for there, where in everyone:
        @pl.when(there)
        def _():
            pl.semaphore_signal(barrier, inc=1, device_id=where, device_id_type=pl.DeviceIdType.MESH)

        total = total + there.astype(jnp.int32)
    pl.semaphore_wait(barrier, total)

    def copy(src, dst, send, recv, where):
        return pltpu.make_async_remote_copy(
            src_ref=src, dst_ref=dst, send_sem=send_sem.at[send], recv_sem=recv_sem.at[recv],
            device_id=where, device_id_type=pl.DeviceIdType.MESH,
        )

    def arrived(dst, recv):
        copy(dst, dst, 0, recv, partner).wait_recv()

    c_a = copy(a_ref, a_oth, 0, R_A, partner)
    c_a.start()
    for load in loads:
        load.wait()

    def stacked(which):
        first, second = pack(e_own[0], e_own[1])
        return jnp.where(which == 0, first, second)

    e_send[...] = stacked(1 - r)
    c_e = copy(e_send, es.at[pl.ds(mine, H), :], 1, R_E, partner)
    c_e.start()
    es[pl.ds(mine, H), :] = stacked(r)

    @pl.loop(0, N // 64)
    def _(t):
        s0 = pl.multiple_of(t * 64, 64)
        hit = lax.broadcasted_iota(jnp.int32, (64, N), 0) + s0 == t_own[...]
        onehot[pl.ds(s0, 64), :] = hit.astype(F32).astype(BF16)

    def twist(i):
        which = 1 - role // 2 if i == 0 else role // 2
        keep = jnp.where(which == 0, slab > 0, slab < slabs - 1).astype(F32)

        @pl.loop(0, 2)
        def _(t):
            high, low = halves(lu_own[which, t])
            tw[i, t] = (dot(high, onehot[...]) + dot(low, onehot[...])) * keep

    twist(0)

    def sender(first):
        count = [first]
        pending = []

        def prepare(make, n=1, when=None):
            base = count[0]
            count[0] += n
            assert count[0] <= N_SEND
            pending.append((make, base, n, when))

            def start(j=0):
                if when is None:
                    make(j, base + j).start()
                else:
                    pl.when(when)(lambda: make(j, base + j).start())

            return start

        def finish():
            for make, base, n, when in pending:
                def wait(make=make, base=base, n=n):
                    for j in range(n):
                        make(j, base + j).wait_send()

                if when is None:
                    wait()
                else:
                    pl.when(when)(wait)

        return prepare, finish

    @pl.when(odd)
    def _():
        is_b = role == 1
        inner = (jnp.where(is_b, plus, minus), r)
        outer = (jnp.where(is_b, minus, plus), r)
        sibling = (jnp.where(is_b, slab_at(-4), slab_at(4)), r)
        has_outer = has_plus
        has_sibling = jnp.where(is_b, slab >= 4, slab < slabs - 4)
        has_second = jnp.logical_or(jnp.logical_not(is_b), slab < slabs - 4)
        side = jnp.where(is_b, 0, 1)
        prepare, finish = sender(2)

        s_ci = prepare(lambda j, s: copy(st_send.at[0], x_ci.at[:, pl.ds(mine, H), :], s, R_CI, partner))
        s_co = prepare(lambda j, s: copy(st_send.at[1], x_co.at[:, pl.ds(mine, H), :], s, R_CO, partner))
        s_yci = prepare(lambda j, s: copy(x_ci.at[j], yin.at[side, j], s, R_YIN + 4 * side + j, inner), C)
        s_ycip = prepare(lambda j, s: copy(x_ci.at[j], y_oth.at[j], s, R_YCI + j, partner), C)
        s_ye = prepare(lambda j, s: copy(ye, yein.at[side], s, R_YE + side, inner))
        s_yco = prepare(lambda j, s: copy(x_co.at[j], wco.at[side, j], s, R_YCO + 4 * side + j, inner), C)
        s_d = prepare(lambda j, s: copy(d_own.at[j], d_oth.at[j], s, R_DP + j, partner), C)
        s_p = prepare(lambda j, s: copy(p_own.at[j], yin.at[side, j], s, R_YIN + 4 * side + j, outer), C, has_outer)
        s_pp = prepare(lambda j, s: copy(p_own.at[j], p_oth.at[j], s, R_P + j, partner), C)
        s_q = prepare(lambda j, s: copy(qv, yein.at[side], s, R_YE + side, outer), 1, has_outer)
        s_r = prepare(lambda j, s: copy(r_own.at[j], r_oth.at[j], s, R_R + j, partner), C)

        def piece(ref, j):
            return ref.at[pl.ds(j * (N // K), N // K), :]

        s_in = prepare(lambda j, s: copy(piece(sin.at[0], j), piece(sin.at[side], j), s, R_S + K * side + j, inner), K, has_outer)
        s_sib = prepare(lambda j, s: copy(piece(sin.at[0], j), piece(sin.at[1], j), s, R_S + K + j, sibling), K, has_sibling)

        stack_rows(st_send.at[0], 0, tw.at[0], other, 0.2)
        s_ci()
        stack_rows(x_ci, mine, tw.at[0], mine, 0.2)
        split_rows(lhs.at[0], a_own, mine, True, 3)
        arrived(a_oth, R_A)
        split_rows(lhs.at[0], a_oth, other, True, 3)
        square(lhs.at[0], lhs.at[1])
        arrived(x_ci.at[:, pl.ds(other, H), :], R_CI)

        @pl.loop(0, C)
        def _(j):
            series(lhs, x_ci.at[j], x_ci.at[j], va, vb)
            s_yci(j)
            s_ycip(j)

        twist(1)
        stack_rows(st_send.at[1], 0, tw.at[1], other, 0.2)
        s_co()
        stack_rows(x_co, mine, tw.at[1], mine, 0.2)
        arrived(x_co.at[:, pl.ds(other, H), :], R_CO)

        @pl.loop(0, C)
        def _(j):
            series(lhs, x_co.at[j], x_co.at[j], va, vb)
            s_yco(j)

        arrived(es.at[pl.ds(other, H), :], R_E)
        ye[...] = 0.2 * es[...]
        series(lhs, ye, ye, va, vb)
        s_ye()
        split_chunks(lc.at[1], x_ci, mine, False, 2)
        for j in range(C):
            arrived(y_oth.at[j], R_YCI + j)
        split_chunks(lc.at[1], y_oth, other, False, 2)
        for j in range(C):
            arrived(d_own.at[j], R_D + j)
            s_d(j)
        split_chunks(lhs.at[0], d_own, mine, True, 3)
        for j in range(C):
            arrived(d_oth.at[j], R_DP + j)
        split_chunks(lhs.at[0], d_oth, other, True, 3)
        square(lhs.at[0], lhs.at[1])

        @pl.loop(0, C)
        def _(j):
            arrived(x_w.at[j], R_W + j)
            series(lhs, x_w.at[j], x_w.at[j], va, vb)
            put(p_own.at[j], lc.at[1], x_w.at[j], x_co.at[j])
            s_p(j)
            s_pp(j)

        arrived(zb, R_ZB)
        put(qv, lc.at[1], zb, ye, -1.0)
        s_q()
        split_chunks(lc.at[2], p_own, mine, False, 2)
        for j in range(C):
            arrived(p_oth.at[j], R_P + j)
        split_chunks(lc.at[2], p_oth, other, False, 2)

        @pl.loop(0, C)
        def _(j):
            arrived(zwx.at[j], R_ZWX + j)
            put(r_own.at[j], lc.at[1], zwx.at[j])
            s_r(j)

        split_chunks(lc.at[0], r_own, mine, False, 2)
        for j in range(C):
            arrived(r_oth.at[j], R_R + j)
        split_chunks(lc.at[0], r_oth, other, False, 2)

        res[...] = qv[...]

        @pl.when(has_outer)
        def _():
            for j in range(K):
                arrived(piece(sin.at[0], j), R_S + j)
                s_in(j)
                s_sib(j)
            put(res, lc.at[2], sin.at[0], res, -1.0)

        @pl.when(has_second)
        def _():
            for j in range(K):
                arrived(piece(sin.at[1], j), R_S + K + j)
            put(res, lc.at[0], sin.at[1], res, -1.0)

        finish()

    @pl.when(jnp.logical_not(odd))
    def _():
        is_c = role == 2
        sides = ((jnp.where(is_c, minus, plus), r), (jnp.where(is_c, plus, minus), r))
        prepare, finish = sender(2)
        prepare_c, finish_c = sender(24)
        prepare_a, finish_a = sender(24)

        def piece(ref, j):
            return ref.at[pl.ds(j * (N // K), N // K), :]

        s_t = prepare(lambda j, s: copy(tw.at[j], tw_oth.at[j], s, R_T + j, partner), 2)
        s_d = prepare(lambda j, s: copy(d_own.at[j], d_oth.at[j], s, R_DP + j, partner), C)
        s_dc = [prepare_c(lambda j, s, i=i: copy(d_own.at[j], d_own.at[j], s, R_D + j, sides[i]), C) for i in range(2)]
        s_w = [prepare_c(lambda j, s, i=i: copy(wco.at[i, j], x_w.at[j], s, R_W + j, sides[i]), C) for i in range(2)]
        s_zb = [prepare_c(lambda j, s, i=i: copy(zb, zb, s, R_ZB, sides[i])) for i in range(2)]
        def pair(ref, m):
            return ref.at[m % 2, m // 2]

        def opposite(m):
            return (jnp.where(m % 2 == 0, sides[1][0], sides[0][0]), r)

        s_zwp = prepare_c(lambda m, s: copy(pair(yin, m), pair(zwo, m), s, R_ZWP + m, partner), 2 * C)
        s_zwx = prepare_c(lambda m, s: copy(pair(yin, m), zwx.at[m // 2], s, R_ZWX + m // 2, opposite(m)), 2 * C)
        place = jnp.where(slab == 0, 1, 0)
        below = (jnp.where(slab == 0, slab_at(3), minus), r)
        s_sa = [
            prepare_a(lambda j, s: copy(piece(zb, j), piece(sin.at[0], j), s, R_S + j, sides[0]), K),
            prepare_a(lambda j, s: copy(piece(zb, j), piece(sin.at[place], j), s, R_S + K * place + j, below), K),
        ]

        twist(1)
        for i in range(2):
            s_t(i)
            split_rows(lc.at[i], tw.at[i], mine, False, 2)

        stack_rows(a_st, mine, a_own, mine, 1.0)
        arrived(a_oth, R_A)
        stack_rows(a_st, other, a_oth, mine, 1.0)
        for i in range(2):
            arrived(tw_oth.at[i], R_T + i)
            split_rows(lc.at[i], tw_oth.at[i], other, False, 2)
        arrived(es.at[pl.ds(other, H), :], R_E)

        @pl.loop(0, C)
        def _(j):
            arrived(yin.at[0, j], R_YIN + j)
            put(d_own.at[j], lc.at[0], yin.at[0, j], a_st.at[j], -1.0)

            @pl.when(has_minus)
            def _():
                arrived(yin.at[1, j], R_YIN + 4 + j)
                put(d_own.at[j], lc.at[1], yin.at[1, j], d_own.at[j], -1.0)

            @pl.when(is_c)
            def _():
                for i in range(2):
                    s_dc[i](j)

            s_d(j)

        split_chunks(lhs.at[0], d_own, mine, True, 3)
        for j in range(C):
            arrived(d_oth.at[j], R_DP + j)
        split_chunks(lhs.at[0], d_oth, other, True, 3)

        def couple(j):
            for i in range(2):
                arrived(wco.at[i, j], R_YCO + 4 * i + j)
                put(wco.at[i, j], lc.at[i], wco.at[i, j], scale=0.2)
                s_w[i](j)

        def inverted(m):
            series(lhs, pair(wco, m), pair(yin, m), va, vb)
            s_zwp(m)

        @pl.when(is_c)
        def _():
            couple(0)

        square(lhs.at[0], lhs.at[1])

        @pl.when(is_c)
        def _():
            @pl.loop(1, C)
            def _(j):
                couple(j)
                inverted(j - 1)

            s_zwx(0)
            s_zwx(1)

        for i in range(2):
            @pl.when(slab >= i)
            def _():
                arrived(yein.at[i], R_YE + i)
                put(es, lc.at[i], yein.at[i], es, -1.0)

        zb[...] = 0.2 * es[...]

        def send_tile(t):
            @pl.when(jnp.logical_not(is_c))
            def _():
                for j in range(t * K // 2, (t + 1) * K // 2):
                    for i in range(2):
                        s_sa[i](j)

        series(lhs, zb, zb, va, vb, send_tile)

        @pl.when(is_c)
        def _():
            for i in range(2):
                s_zb[i]()

            s_zwx(2)

            @pl.loop(C - 1, 2 * C)
            def _(m):
                inverted(m)
                s_zwx(m)

            for i in range(2):
                split_chunks(lc.at[i], yin.at[i], mine, False, 2)
            for i in range(2):
                for j in range(C):
                    arrived(zwo.at[i, j], R_ZWP + 2 * j + i)
                split_chunks(lc.at[i], zwo.at[i], other, False, 2)
            res[...] = zb[...]
            for i in range(2):
                @pl.when(slab < slabs - 1 - i)
                def _():
                    for j in range(K):
                        arrived(piece(sin.at[i], j), R_S + K * i + j)
                    put(res, lc.at[i], sin.at[i], res)

            finish_c()

        @pl.when(jnp.logical_not(is_c))
        def _():
            res[...] = zb[...]
            finish_a()

        finish()

    c_f = copy(res.at[pl.ds(other, H), :], fin, N_SEND, R_FIN, partner)
    c_f.start()
    own = res[pl.ds(mine, H), :]
    arrived(fin, R_FIN)
    oth = fin[...]
    re, im = unpack(jnp.where(r == 0, own, oth), jnp.where(r == 0, oth, own))
    o_ref[0] = re
    o_ref[1] = im
    c_f.wait_send()
    c_a.wait_send()
    c_e.wait_send()


def solution(mesh):
    slabs = mesh.shape["slab"]

    def body(diag_block, lower_block, upper_block, twist, excitation):
        vmem = pl.BlockSpec(memory_space=pltpu.VMEM)

        def f32(*shape):
            return pltpu.VMEM(shape, F32)

        rows, chunks, vector = f32(2, H, N), f32(C, N, Q), f32(N, Q)
        out = pl.pallas_call(
            functools.partial(kernel, slabs),
            out_shape=jax.ShapeDtypeStruct((2, H, Q), F32),
            in_specs=[pl.BlockSpec(memory_space=pl.ANY)] * 5,
            out_specs=vmem,
            scratch_shapes=[
                rows, f32(2, 2, H, N), f32(2, H, Q),
                pltpu.VMEM((1, N), jnp.int32),
                pltpu.VMEM((N, N), BF16),
                f32(2, 2, H, N), rows, f32(2, 2, H, N),
                chunks, f32(2, C, H, Q),
                chunks, chunks, chunks, chunks,
                f32(2, C, N, Q),
                chunks, chunks, chunks, chunks,
                chunks, chunks, chunks,
                f32(2, C, N, Q), f32(2, C, N, Q), f32(2, N, Q),
                vector, f32(H, Q),
                vector, vector, vector, vector, vector, vector,
                f32(2, N, Q), f32(H, Q),
                pltpu.VMEM((2, 3, 2, N, N), BF16),
                pltpu.VMEM((3, 2, 2, N, N), BF16),
                pltpu.SemaphoreType.DMA((N_SEND + 1,)),
                pltpu.SemaphoreType.DMA((N_RECV,)),
                pltpu.SemaphoreType.DMA((5,)),
            ],
            compiler_params=pltpu.CompilerParams(
                collective_id=0, has_side_effects=True, vmem_limit_bytes=60 * 1024 * 1024
            ),
        )(diag_block[0], lower_block[0], upper_block[0], twist, excitation[0])
        return out[None]

    spec = P("slab", None, "row", None)
    return jax.shard_map(
        body,
        mesh=mesh,
        in_specs=(spec, spec, spec, P("slab", None), spec),
        out_specs=spec,
        check_vma=False,
    )
```

```python
import functools

import jax
import jax.numpy as jnp
from jax import lax
from jax.experimental import pallas as pl
from jax.experimental.pallas import tpu as pltpu
from jax.sharding import PartitionSpec as P

F32 = jnp.float32
BF16 = jnp.bfloat16
N = 512
H = 256
Q = 128
C = 4
K = 8

R_A, R_E, R_T, R_CI, R_CO, R_FIN, R_ZB = 0, 1, 2, 4, 5, 8, 9
R_YE = 10
R_YCI, R_D, R_DP, R_P, R_R, R_ZWX = 12, 16, 20, 24, 28, 32
R_YIN, R_ZWP, R_S = 36, 52, 60
R_W, R_YCO = 76, 80
N_RECV = 88
N_SEND = 72


def dot(a, b):
    return jnp.dot(a, b, preferred_element_type=F32)


def halves(x):
    high = x.astype(BF16)
    return high, (x - high.astype(F32)).astype(BF16)


def put_split(dst, rs, cs, re, im, planes):
    for plane, value in enumerate((re, im, re + im)[:planes]):
        high, low = halves(value)
        dst[plane, 0, rs, cs] = high
        dst[plane, 1, rs, cs] = low


def product3(lhs, rs, rhs, cs):
    parts = []
    for plane in range(3):
        ah, al = lhs[plane, 0, rs, :], lhs[plane, 1, rs, :]
        bh, bl = rhs[plane, 0, :, cs], rhs[plane, 1, :, cs]
        parts.append(dot(ah, bh) + dot(ah, bl) + dot(al, bh))
    return parts[0] - parts[1], parts[2] - parts[0] - parts[1]


def lane_low(shape):
    return lax.broadcasted_iota(jnp.int32, shape, 1) < Q // 2


def turn(x):
    return pltpu.roll(x, Q // 2, 1)


def pack(re, im):
    low = lane_low(re.shape)
    return jnp.where(low, re, turn(im)), jnp.where(low, turn(re), im)


def unpack(first, second):
    low = lane_low(first.shape)
    return jnp.where(low, first, turn(second)), jnp.where(low, turn(first), second)


def vector_product(lhs, stack_ref, emit, flip=None):
    high, low = halves(stack_ref[...])
    both = jnp.concatenate([high, low], axis=1)
    for t in range(N // H):
        rs = pl.ds(t * H if flip is None else pl.multiple_of((t + flip) % 2 * H, H), H)
        out = []
        for plane in range(2):
            wide = dot(lhs[plane, 0, rs, :], both)
            out.append(wide[:, :Q] + wide[:, Q:] + dot(lhs[plane, 1, rs, :], high))
        turned = turn(out[1])
        emit(t, rs, out[0] + jnp.where(lane_low((H, Q)), -turned, turned))


def put(dst, lhs, src, base=None, scale=1.0, ready=None, flip=None):
    def emit(t, rs, value):
        value = value if scale == 1.0 else scale * value
        dst[rs, :] = value if base is None else base[rs, :] + value
        if ready is not None:
            ready(t)

    vector_product(lhs, src, emit, flip)


def identity_minus(re, im, row0, col0):
    eye = (
        lax.broadcasted_iota(jnp.int32, re.shape, 0) + row0 == lax.broadcasted_iota(jnp.int32, re.shape, 1) + col0
    ).astype(F32)
    return eye - 0.2 * re, -0.2 * im


def split_rows(dst, src, row0, inverse, planes):
    @pl.loop(0, H // 32)
    def _(t):
        s0 = pl.multiple_of(t * 32, 32)
        d0 = pl.multiple_of(row0 + s0, 32)
        re, im = src[0, pl.ds(s0, 32), :], src[1, pl.ds(s0, 32), :]
        if inverse:
            re, im = identity_minus(re, im, d0, 0)
        put_split(dst, pl.ds(d0, 32), slice(None), re, im, planes)


def split_chunks(dst, src, col0, inverse, planes):
    @pl.loop(0, N // 32)
    def _(t):
        rs = pl.ds(pl.multiple_of(t * 32, 32), 32)
        for m in range(C // 2):
            c0 = pl.multiple_of(col0 + m * Q, Q)
            re, im = unpack(src[2 * m, rs, :], src[2 * m + 1, rs, :])
            if inverse:
                re, im = identity_minus(re, im, t * 32, c0)
            put_split(dst, rs, pl.ds(c0, Q), re, im, planes)


def stack_rows(dst, dst_row0, src, col0, scale):
    @pl.loop(0, H // 32)
    def _(t):
        rs = pl.ds(pl.multiple_of(t * 32, 32), 32)
        ds = pl.ds(pl.multiple_of(dst_row0 + t * 32, 32), 32)
        for m in range(C // 2):
            cs = pl.ds(pl.multiple_of(col0 + m * Q, Q), Q)
            first, second = pack(src[0, rs, cs], src[1, rs, cs])
            dst[2 * m, ds, :] = scale * first
            dst[2 * m + 1, ds, :] = scale * second


def square(src, dst):
    @pl.loop(0, 4)
    def _(t):
        rs = pl.ds(pl.multiple_of((t // 2) * H, H), H)
        cs = pl.ds(pl.multiple_of((t % 2) * H, H), H)
        re, im = product3(src, rs, src, cs)
        put_split(dst, rs, cs, re, im, 2)


def series(lhs, src, dst, va, vb, ready=None):
    put(va, lhs.at[0], src, src)
    put(vb, lhs.at[1], va, va)
    put(va, lhs.at[1], vb)
    put(dst, lhs.at[1], va, vb, ready=ready)


def kernel(
    slabs,
    a_ref, l_ref, u_ref, tw_ref, e_ref, o_ref,
    a_own, lu_own, e_own, t_own, onehot, tw, a_oth, tw_oth, a_st, st_send, x_ci, x_co, x_w, y_oth, wco,
    d_own, d_oth, p_own, p_oth, zwx, r_own, r_oth, yin, zwo, yein, es, e_send,
    va, vb, ye, zb, qv, res, sin, fin, lhs, lc, send_sem, recv_sem, load_sem,
):
    slab = lax.axis_index("slab")
    r = lax.axis_index("row")
    role = lax.rem(slab, 4)
    odd = lax.rem(role, 2) == 1

    loads = []
    for k, (src, dst) in enumerate(((a_ref, a_own), (tw_ref, t_own), (l_ref, lu_own.at[0]), (u_ref, lu_own.at[1]), (e_ref, e_own))):
        load = pltpu.make_async_copy(src, dst, load_sem.at[k])
        load.start()
        loads.append(load)

    def slab_at(offset):
        return lax.rem(slab + slabs + offset, slabs)

    plus, minus = slab_at(1), slab_at(-1)
    has_plus, has_minus = slab < slabs - 1, slab > 0
    mine = pl.multiple_of(r * H, H)
    other = pl.multiple_of((1 - r) * H, H)
    partner = (slab, 1 - r)

    barrier = pltpu.get_barrier_semaphore()
    everyone = (
        (slab >= 0, partner),
        (has_plus, (plus, r)),
        (has_minus, (minus, r)),
        (jnp.logical_and(odd, slab >= 4), (slab_at(-4), r)),
        (jnp.logical_and(odd, slab < slabs - 4), (slab_at(4), r)),
        (slab == 0, (slab_at(3), r)),
        (slab == 3, (slab_at(-3), r)),
    )
    total = 0
    for there, where in everyone:
        @pl.when(there)
        def _():
            pl.semaphore_signal(barrier, inc=1, device_id=where, device_id_type=pl.DeviceIdType.MESH)

        total = total + there.astype(jnp.int32)
    pl.semaphore_wait(barrier, total)

    def copy(src, dst, send, recv, where):
        return pltpu.make_async_remote_copy(
            src_ref=src, dst_ref=dst, send_sem=send_sem.at[send], recv_sem=recv_sem.at[recv],
            device_id=where, device_id_type=pl.DeviceIdType.MESH,
        )

    def arrived(dst, recv):
        copy(dst, dst, 0, recv, partner).wait_recv()

    c_a = copy(a_ref, a_oth, 0, R_A, partner)
    c_a.start()
    for load in loads:
        load.wait()

    def stacked(which):
        first, second = pack(e_own[0], e_own[1])
        return jnp.where(which == 0, first, second)

    e_send[...] = stacked(1 - r)
    c_e = copy(e_send, es.at[pl.ds(mine, H), :], 1, R_E, partner)
    c_e.start()
    es[pl.ds(mine, H), :] = stacked(r)

    @pl.loop(0, N // 64)
    def _(t):
        s0 = pl.multiple_of(t * 64, 64)
        hit = lax.broadcasted_iota(jnp.int32, (64, N), 0) + s0 == t_own[...]
        onehot[pl.ds(s0, 64), :] = hit.astype(F32).astype(BF16)

    def twist(i):
        which = 1 - role // 2 if i == 0 else role // 2
        keep = jnp.where(which == 0, slab > 0, slab < slabs - 1).astype(F32)

        @pl.loop(0, 2)
        def _(t):
            high, low = halves(lu_own[which, t])
            tw[i, t] = (dot(high, onehot[...]) + dot(low, onehot[...])) * keep

    twist(0)

    c_f = copy(res.at[pl.ds(other, H), :], fin, N_SEND, R_FIN, partner)
    early = jnp.where(odd, jnp.logical_or(role == 3, slab < slabs - 4), jnp.logical_and(role == 2, slab < slabs - 2))

    def hand_over(t):
        if t == 0:
            c_f.start()

    def sender(first):
        count = [first]
        pending = []

        def prepare(make, n=1, when=None):
            base = count[0]
            count[0] += n
            assert count[0] <= N_SEND
            pending.append((make, base, n, when))

            def start(j=0):
                if when is None:
                    make(j, base + j).start()
                else:
                    pl.when(when)(lambda: make(j, base + j).start())

            return start

        def finish():
            for make, base, n, when in pending:
                def wait(make=make, base=base, n=n):
                    for j in range(n):
                        make(j, base + j).wait_send()

                if when is None:
                    wait()
                else:
                    pl.when(when)(wait)

        return prepare, finish

    @pl.when(odd)
    def _():
        is_b = role == 1
        inner = (jnp.where(is_b, plus, minus), r)
        outer = (jnp.where(is_b, minus, plus), r)
        sibling = (jnp.where(is_b, slab_at(-4), slab_at(4)), r)
        has_outer = has_plus
        has_sibling = jnp.where(is_b, slab >= 4, slab < slabs - 4)
        has_second = jnp.logical_or(jnp.logical_not(is_b), slab < slabs - 4)
        side = jnp.where(is_b, 0, 1)
        prepare, finish = sender(2)

        s_ci = prepare(lambda j, s: copy(st_send.at[0], x_ci.at[:, pl.ds(mine, H), :], s, R_CI, partner))
        s_co = prepare(lambda j, s: copy(st_send.at[1], x_co.at[:, pl.ds(mine, H), :], s, R_CO, partner))
        s_yci = prepare(lambda j, s: copy(x_ci.at[j], yin.at[side, j], s, R_YIN + 4 * side + j, inner), C)
        s_ycip = prepare(lambda j, s: copy(x_ci.at[j], y_oth.at[j], s, R_YCI + j, partner), C)
        s_ye = prepare(lambda j, s: copy(ye, yein.at[side], s, R_YE + side, inner))
        s_yco = prepare(lambda j, s: copy(x_co.at[j], wco.at[side, j], s, R_YCO + 4 * side + j, inner), C)
        s_d = prepare(lambda j, s: copy(d_own.at[j], d_oth.at[j], s, R_DP + j, partner), C)
        s_p = prepare(lambda j, s: copy(p_own.at[j], yin.at[side, j], s, R_YIN + 4 * side + j, outer), C, has_outer)
        s_pp = prepare(lambda j, s: copy(p_own.at[j], p_oth.at[j], s, R_P + j, partner), C)
        s_q = prepare(lambda j, s: copy(qv, yein.at[side], s, R_YE + side, outer), 1, has_outer)
        s_r = prepare(lambda j, s: copy(r_own.at[j], r_oth.at[j], s, R_R + j, partner), C)

        def piece(ref, j):
            return ref.at[pl.ds(j * (N // K), N // K), :]

        s_in = prepare(lambda j, s: copy(piece(sin.at[0], j), piece(sin.at[side], j), s, R_S + K * side + j, inner), K, has_outer)
        s_sib = prepare(lambda j, s: copy(piece(sin.at[0], j), piece(sin.at[1], j), s, R_S + K + j, sibling), K, has_sibling)

        stack_rows(st_send.at[0], 0, tw.at[0], other, 0.2)
        s_ci()
        stack_rows(x_ci, mine, tw.at[0], mine, 0.2)
        split_rows(lhs.at[0], a_own, mine, True, 3)
        arrived(a_oth, R_A)
        split_rows(lhs.at[0], a_oth, other, True, 3)
        square(lhs.at[0], lhs.at[1])
        arrived(x_ci.at[:, pl.ds(other, H), :], R_CI)

        @pl.loop(0, C)
        def _(j):
            series(lhs, x_ci.at[j], x_ci.at[j], va, vb)
            s_yci(j)
            s_ycip(j)

        twist(1)
        stack_rows(st_send.at[1], 0, tw.at[1], other, 0.2)
        s_co()
        stack_rows(x_co, mine, tw.at[1], mine, 0.2)
        arrived(x_co.at[:, pl.ds(other, H), :], R_CO)

        @pl.loop(0, C)
        def _(j):
            series(lhs, x_co.at[j], x_co.at[j], va, vb)
            s_yco(j)

        arrived(es.at[pl.ds(other, H), :], R_E)
        ye[...] = 0.2 * es[...]
        series(lhs, ye, ye, va, vb)
        s_ye()
        split_chunks(lc.at[1], x_ci, mine, False, 2)
        for j in range(C):
            arrived(y_oth.at[j], R_YCI + j)
        split_chunks(lc.at[1], y_oth, other, False, 2)
        for j in range(C):
            arrived(d_own.at[j], R_D + j)
            s_d(j)
        split_chunks(lhs.at[0], d_own, mine, True, 3)
        for j in range(C):
            arrived(d_oth.at[j], R_DP + j)
        split_chunks(lhs.at[0], d_oth, other, True, 3)
        square(lhs.at[0], lhs.at[1])

        @pl.loop(0, C)
        def _(j):
            arrived(x_w.at[j], R_W + j)
            series(lhs, x_w.at[j], x_w.at[j], va, vb)
            put(p_own.at[j], lc.at[1], x_w.at[j], x_co.at[j])
            s_p(j)
            s_pp(j)

        arrived(zb, R_ZB)
        put(qv, lc.at[1], zb, ye, -1.0)
        s_q()
        split_chunks(lc.at[2], p_own, mine, False, 2)
        for j in range(C):
            arrived(p_oth.at[j], R_P + j)
        split_chunks(lc.at[2], p_oth, other, False, 2)

        def second(j):
            arrived(zwx.at[j], R_ZWX + j)
            put(r_own.at[j], lc.at[1], zwx.at[j])
            s_r(j)

        def relay(first, last):
            @pl.when(has_outer)
            def _():
                for j in range(first, last):
                    arrived(piece(sin.at[0], j), R_S + j)
                    s_in(j)
                    s_sib(j)

        pl.loop(0, C - 1)(second)
        relay(0, K // 2)
        second(C - 1)
        relay(K // 2, K)
        split_chunks(lc.at[0], r_own, mine, False, 2)
        res[...] = qv[...]

        @pl.when(has_outer)
        def _():
            put(res, lc.at[2], sin.at[0], res, -1.0)

        for j in range(C):
            arrived(r_oth.at[j], R_R + j)
        split_chunks(lc.at[0], r_oth, other, False, 2)

        @pl.when(has_second)
        def _():
            for j in range(K):
                arrived(piece(sin.at[1], j), R_S + K + j)
            put(res, lc.at[0], sin.at[1], res, -1.0, hand_over, 1 - r)

        finish()

    @pl.when(jnp.logical_not(odd))
    def _():
        is_c = role == 2
        sides = ((jnp.where(is_c, minus, plus), r), (jnp.where(is_c, plus, minus), r))
        prepare, finish = sender(2)
        prepare_c, finish_c = sender(24)
        prepare_a, finish_a = sender(24)

        def piece(ref, j):
            return ref.at[pl.ds(j * (N // K), N // K), :]

        s_t = prepare(lambda j, s: copy(tw.at[j], tw_oth.at[j], s, R_T + j, partner), 2)
        s_d = prepare(lambda j, s: copy(d_own.at[j], d_oth.at[j], s, R_DP + j, partner), C)
        s_dc = [prepare_c(lambda j, s, i=i: copy(d_own.at[j], d_own.at[j], s, R_D + j, sides[i]), C) for i in range(2)]
        s_w = [prepare_c(lambda j, s, i=i: copy(wco.at[i, j], x_w.at[j], s, R_W + j, sides[i]), C) for i in range(2)]
        s_zb = [prepare_c(lambda j, s, i=i: copy(zb, zb, s, R_ZB, sides[i])) for i in range(2)]
        def pair(ref, m):
            return ref.at[m % 2, m // 2]

        def opposite(m):
            return (jnp.where(m % 2 == 0, sides[1][0], sides[0][0]), r)

        s_zwp = prepare_c(lambda m, s: copy(pair(yin, m), pair(zwo, m), s, R_ZWP + m, partner), 2 * C)
        s_zwx = prepare_c(lambda m, s: copy(pair(yin, m), zwx.at[m // 2], s, R_ZWX + m // 2, opposite(m)), 2 * C)
        place = jnp.where(slab == 0, 1, 0)
        below = (jnp.where(slab == 0, slab_at(3), minus), r)
        s_sa = [
            prepare_a(lambda j, s: copy(piece(zb, j), piece(sin.at[0], j), s, R_S + j, sides[0]), K),
            prepare_a(lambda j, s: copy(piece(zb, j), piece(sin.at[place], j), s, R_S + K * place + j, below), K),
        ]

        twist(1)
        for i in range(2):
            s_t(i)
            split_rows(lc.at[i], tw.at[i], mine, False, 2)

        stack_rows(a_st, mine, a_own, mine, 1.0)
        arrived(a_oth, R_A)
        stack_rows(a_st, other, a_oth, mine, 1.0)
        for i in range(2):
            arrived(tw_oth.at[i], R_T + i)
            split_rows(lc.at[i], tw_oth.at[i], other, False, 2)
        arrived(es.at[pl.ds(other, H), :], R_E)

        @pl.loop(0, C)
        def _(j):
            arrived(yin.at[0, j], R_YIN + j)
            put(d_own.at[j], lc.at[0], yin.at[0, j], a_st.at[j], -1.0)

            @pl.when(has_minus)
            def _():
                arrived(yin.at[1, j], R_YIN + 4 + j)
                put(d_own.at[j], lc.at[1], yin.at[1, j], d_own.at[j], -1.0)

            @pl.when(is_c)
            def _():
                for i in range(2):
                    s_dc[i](j)

            s_d(j)

        split_chunks(lhs.at[0], d_own, mine, True, 3)
        for j in range(C):
            arrived(d_oth.at[j], R_DP + j)
        split_chunks(lhs.at[0], d_oth, other, True, 3)

        def couple(j):
            for i in range(2):
                arrived(wco.at[i, j], R_YCO + 4 * i + j)
                put(wco.at[i, j], lc.at[i], wco.at[i, j], scale=0.2)
                s_w[i](j)

        def inverted(m):
            series(lhs, pair(wco, m), pair(yin, m), va, vb)
            s_zwp(m)

        @pl.when(is_c)
        def _():
            couple(0)

        square(lhs.at[0], lhs.at[1])

        @pl.when(is_c)
        def _():
            @pl.loop(1, C)
            def _(j):
                couple(j)
                inverted(j - 1)

            s_zwx(0)
            s_zwx(1)

        for i in range(2):
            @pl.when(slab >= i)
            def _():
                arrived(yein.at[i], R_YE + i)
                put(es, lc.at[i], yein.at[i], es, -1.0)

        zb[...] = 0.2 * es[...]

        def send_tile(t):
            @pl.when(jnp.logical_not(is_c))
            def _():
                for j in range(t * K // 2, (t + 1) * K // 2):
                    for i in range(2):
                        s_sa[i](j)

        series(lhs, zb, zb, va, vb, send_tile)

        @pl.when(is_c)
        def _():
            for i in range(2):
                s_zb[i]()

            s_zwx(2)

            @pl.loop(C - 1, 2 * C)
            def _(m):
                inverted(m)
                s_zwx(m)

            for i in range(2):
                split_chunks(lc.at[i], yin.at[i], mine, False, 2)
            for i in range(2):
                for j in range(C):
                    arrived(zwo.at[i, j], R_ZWP + 2 * j + i)
                split_chunks(lc.at[i], zwo.at[i], other, False, 2)
            res[...] = zb[...]
            for i in range(2):
                @pl.when(slab < slabs - 1 - i)
                def _():
                    for j in range(K):
                        arrived(piece(sin.at[i], j), R_S + K * i + j)
                    put(res, lc.at[i], sin.at[i], res, 1.0, hand_over if i else None, 1 - r)

            finish_c()

        @pl.when(jnp.logical_not(is_c))
        def _():
            res[...] = zb[...]
            finish_a()

        finish()

    pl.when(jnp.logical_not(early))(c_f.start)
    own = res[pl.ds(mine, H), :]
    arrived(fin, R_FIN)
    oth = fin[...]
    re, im = unpack(jnp.where(r == 0, own, oth), jnp.where(r == 0, oth, own))
    o_ref[0] = re
    o_ref[1] = im
    c_f.wait_send()
    c_a.wait_send()
    c_e.wait_send()


def solution(mesh):
    slabs = mesh.shape["slab"]

    def body(diag_block, lower_block, upper_block, twist, excitation):
        vmem = pl.BlockSpec(memory_space=pltpu.VMEM)

        def f32(*shape):
            return pltpu.VMEM(shape, F32)

        rows, chunks, vector = f32(2, H, N), f32(C, N, Q), f32(N, Q)
        out = pl.pallas_call(
            functools.partial(kernel, slabs),
            out_shape=jax.ShapeDtypeStruct((2, H, Q), F32),
            in_specs=[pl.BlockSpec(memory_space=pl.ANY)] * 5,
            out_specs=vmem,
            scratch_shapes=[
                rows, f32(2, 2, H, N), f32(2, H, Q),
                pltpu.VMEM((1, N), jnp.int32),
                pltpu.VMEM((N, N), BF16),
                f32(2, 2, H, N), rows, f32(2, 2, H, N),
                chunks, f32(2, C, H, Q),
                chunks, chunks, chunks, chunks,
                f32(2, C, N, Q),
                chunks, chunks, chunks, chunks,
                chunks, chunks, chunks,
                f32(2, C, N, Q), f32(2, C, N, Q), f32(2, N, Q),
                vector, f32(H, Q),
                vector, vector, vector, vector, vector, vector,
                f32(2, N, Q), f32(H, Q),
                pltpu.VMEM((2, 3, 2, N, N), BF16),
                pltpu.VMEM((3, 2, 2, N, N), BF16),
                pltpu.SemaphoreType.DMA((N_SEND + 1,)),
                pltpu.SemaphoreType.DMA((N_RECV,)),
                pltpu.SemaphoreType.DMA((5,)),
            ],
            compiler_params=pltpu.CompilerParams(
                collective_id=0, has_side_effects=True, vmem_limit_bytes=60 * 1024 * 1024
            ),
        )(diag_block[0], lower_block[0], upper_block[0], twist, excitation[0])
        return out[None]

    spec = P("slab", None, "row", None)
    return jax.shard_map(
        body,
        mesh=mesh,
        in_specs=(spec, spec, spec, P("slab", None), spec),
        out_specs=spec,
        check_vma=False,
    )
```

```python
import functools

import jax
import jax.numpy as jnp
from jax import lax
from jax.experimental import pallas as pl
from jax.experimental.pallas import tpu as pltpu
from jax.sharding import PartitionSpec as P

F32 = jnp.float32
BF16 = jnp.bfloat16
N = 512
H = 256
Q = 128
C = 4
K = 4

R_A, R_E, R_T, R_CI, R_CO, R_FIN, R_ZB = 0, 1, 2, 4, 5, 8, 9
R_YE = 10
R_YCI, R_D, R_DP, R_P, R_R, R_ZWX = 12, 16, 20, 24, 28, 32
R_YIN, R_ZWP, R_S = 36, 52, 60
R_W, R_YCO = 76, 80
N_RECV = 88
N_SEND = 72


def dot(a, b):
    return jnp.dot(a, b, preferred_element_type=F32)


def halves(x):
    high = x.astype(BF16)
    return high, (x - high.astype(F32)).astype(BF16)


def put_split(dst, rs, cs, re, im, planes):
    for plane, value in enumerate((re, im, re + im)[:planes]):
        high, low = halves(value)
        dst[plane, 0, rs, cs] = high
        dst[plane, 1, rs, cs] = low


def product3(lhs, rs, rhs, cs):
    parts = []
    for plane in range(3):
        ah, al = lhs[plane, 0, rs, :], lhs[plane, 1, rs, :]
        bh, bl = rhs[plane, 0, :, cs], rhs[plane, 1, :, cs]
        parts.append(dot(ah, bh) + dot(ah, bl) + dot(al, bh))
    return parts[0] - parts[1], parts[2] - parts[0] - parts[1]


def lane_low(shape):
    return lax.broadcasted_iota(jnp.int32, shape, 1) < Q // 2


def turn(x):
    return pltpu.roll(x, Q // 2, 1)


def pack(re, im):
    low = lane_low(re.shape)
    return jnp.where(low, re, turn(im)), jnp.where(low, turn(re), im)


def unpack(first, second):
    low = lane_low(first.shape)
    return jnp.where(low, first, turn(second)), jnp.where(low, turn(first), second)


def vector_product(lhs, stack_ref, emit, flip=None):
    high, low = halves(stack_ref[...])
    both = jnp.concatenate([high, low], axis=1)
    for t in range(N // H):
        rs = pl.ds(t * H if flip is None else pl.multiple_of((t + flip) % 2 * H, H), H)
        out = []
        for plane in range(2):
            wide = dot(lhs[plane, 0, rs, :], both)
            out.append(wide[:, :Q] + wide[:, Q:] + dot(lhs[plane, 1, rs, :], high))
        turned = turn(out[1])
        emit(t, rs, out[0] + jnp.where(lane_low((H, Q)), -turned, turned))


def put(dst, lhs, src, base=None, scale=1.0, ready=None, flip=None):
    def emit(t, rs, value):
        value = value if scale == 1.0 else scale * value
        dst[rs, :] = value if base is None else base[rs, :] + value
        if ready is not None:
            ready(t)

    vector_product(lhs, src, emit, flip)


def identity_minus(re, im, row0, col0):
    eye = (
        lax.broadcasted_iota(jnp.int32, re.shape, 0) + row0 == lax.broadcasted_iota(jnp.int32, re.shape, 1) + col0
    ).astype(F32)
    return eye - 0.2 * re, -0.2 * im


def split_rows(dst, src, row0, inverse, planes):
    @pl.loop(0, H // 32)
    def _(t):
        s0 = pl.multiple_of(t * 32, 32)
        d0 = pl.multiple_of(row0 + s0, 32)
        re, im = src[0, pl.ds(s0, 32), :], src[1, pl.ds(s0, 32), :]
        if inverse:
            re, im = identity_minus(re, im, d0, 0)
        put_split(dst, pl.ds(d0, 32), slice(None), re, im, planes)


def split_chunks(dst, src, col0, inverse, planes):
    @pl.loop(0, N // 32)
    def _(t):
        rs = pl.ds(pl.multiple_of(t * 32, 32), 32)
        for m in range(C // 2):
            c0 = pl.multiple_of(col0 + m * Q, Q)
            re, im = unpack(src[2 * m, rs, :], src[2 * m + 1, rs, :])
            if inverse:
                re, im = identity_minus(re, im, t * 32, c0)
            put_split(dst, rs, pl.ds(c0, Q), re, im, planes)


def stack_rows(dst, dst_row0, src, col0, scale):
    @pl.loop(0, H // 32)
    def _(t):
        rs = pl.ds(pl.multiple_of(t * 32, 32), 32)
        ds = pl.ds(pl.multiple_of(dst_row0 + t * 32, 32), 32)
        for m in range(C // 2):
            cs = pl.ds(pl.multiple_of(col0 + m * Q, Q), Q)
            first, second = pack(src[0, rs, cs], src[1, rs, cs])
            dst[2 * m, ds, :] = scale * first
            dst[2 * m + 1, ds, :] = scale * second


def square(src, dst):
    @pl.loop(0, 4)
    def _(t):
        rs = pl.ds(pl.multiple_of((t // 2) * H, H), H)
        cs = pl.ds(pl.multiple_of((t % 2) * H, H), H)
        re, im = product3(src, rs, src, cs)
        put_split(dst, rs, cs, re, im, 2)


def series(lhs, src, dst, va, vb, ready=None):
    put(va, lhs.at[0], src, src)
    put(vb, lhs.at[1], va, va)
    put(va, lhs.at[1], vb)
    put(dst, lhs.at[1], va, vb, ready=ready)


def kernel(
    slabs,
    a_ref, l_ref, u_ref, tw_ref, e_ref, o_ref,
    a_own, lu_own, e_own, t_own, onehot, tw, a_oth, tw_oth, a_st, st_send, x_ci, x_co, x_w, y_oth, wco,
    d_own, d_oth, p_own, p_oth, zwx, r_own, r_oth, yin, zwo, yein, es, e_send,
    va, vb, ye, zb, qv, res, sin, fin, lhs, lc, send_sem, recv_sem, load_sem,
):
    slab = lax.axis_index("slab")
    r = lax.axis_index("row")
    role = lax.rem(slab, 4)
    odd = lax.rem(role, 2) == 1

    loads = []
    for k, (src, dst) in enumerate(((a_ref, a_own), (tw_ref, t_own), (l_ref, lu_own.at[0]), (u_ref, lu_own.at[1]), (e_ref, e_own))):
        load = pltpu.make_async_copy(src, dst, load_sem.at[k])
        load.start()
        loads.append(load)

    def slab_at(offset):
        return lax.rem(slab + slabs + offset, slabs)

    plus, minus = slab_at(1), slab_at(-1)
    has_plus, has_minus = slab < slabs - 1, slab > 0
    mine = pl.multiple_of(r * H, H)
    other = pl.multiple_of((1 - r) * H, H)
    partner = (slab, 1 - r)

    barrier = pltpu.get_barrier_semaphore()
    everyone = (
        (slab >= 0, partner),
        (has_plus, (plus, r)),
        (has_minus, (minus, r)),
        (jnp.logical_and(odd, slab >= 4), (slab_at(-4), r)),
        (jnp.logical_and(odd, slab < slabs - 4), (slab_at(4), r)),
        (slab == 0, (slab_at(3), r)),
        (slab == 3, (slab_at(-3), r)),
    )
    total = 0
    for there, where in everyone:
        @pl.when(there)
        def _():
            pl.semaphore_signal(barrier, inc=1, device_id=where, device_id_type=pl.DeviceIdType.MESH)

        total = total + there.astype(jnp.int32)
    pl.semaphore_wait(barrier, total)

    def copy(src, dst, send, recv, where):
        return pltpu.make_async_remote_copy(
            src_ref=src, dst_ref=dst, send_sem=send_sem.at[send], recv_sem=recv_sem.at[recv],
            device_id=where, device_id_type=pl.DeviceIdType.MESH,
        )

    def arrived(dst, recv):
        copy(dst, dst, 0, recv, partner).wait_recv()

    c_a = copy(a_ref, a_oth, 0, R_A, partner)
    c_a.start()
    for load in loads:
        load.wait()

    def stacked(which):
        first, second = pack(e_own[0], e_own[1])
        return jnp.where(which == 0, first, second)

    e_send[...] = stacked(1 - r)
    c_e = copy(e_send, es.at[pl.ds(mine, H), :], 1, R_E, partner)
    c_e.start()
    es[pl.ds(mine, H), :] = stacked(r)

    @pl.loop(0, N // 64)
    def _(t):
        s0 = pl.multiple_of(t * 64, 64)
        hit = lax.broadcasted_iota(jnp.int32, (64, N), 0) + s0 == t_own[...]
        onehot[pl.ds(s0, 64), :] = hit.astype(F32).astype(BF16)

    def twist(i):
        which = 1 - role // 2 if i == 0 else role // 2
        keep = jnp.where(which == 0, slab > 0, slab < slabs - 1).astype(F32)

        @pl.loop(0, 2)
        def _(t):
            high, low = halves(lu_own[which, t])
            tw[i, t] = (dot(high, onehot[...]) + dot(low, onehot[...])) * keep

    twist(0)

    c_f = copy(res.at[pl.ds(other, H), :], fin, N_SEND, R_FIN, partner)
    early = jnp.where(odd, jnp.logical_or(role == 3, slab < slabs - 4), jnp.logical_and(role == 2, slab < slabs - 2))

    def hand_over(t):
        if t == 0:
            c_f.start()

    def sender(first):
        count = [first]
        pending = []

        def prepare(make, n=1, when=None):
            base = count[0]
            count[0] += n
            assert count[0] <= N_SEND
            pending.append((make, base, n, when))

            def start(j=0):
                if when is None:
                    make(j, base + j).start()
                else:
                    pl.when(when)(lambda: make(j, base + j).start())

            return start

        def finish():
            for make, base, n, when in pending:
                def wait(make=make, base=base, n=n):
                    for j in range(n):
                        make(j, base + j).wait_send()

                if when is None:
                    wait()
                else:
                    pl.when(when)(wait)

        return prepare, finish

    @pl.when(odd)
    def _():
        is_b = role == 1
        inner = (jnp.where(is_b, plus, minus), r)
        outer = (jnp.where(is_b, minus, plus), r)
        sibling = (jnp.where(is_b, slab_at(-4), slab_at(4)), r)
        has_outer = has_plus
        has_sibling = jnp.where(is_b, slab >= 4, slab < slabs - 4)
        has_second = jnp.logical_or(jnp.logical_not(is_b), slab < slabs - 4)
        side = jnp.where(is_b, 0, 1)
        prepare, finish = sender(2)

        s_ci = prepare(lambda j, s: copy(st_send.at[0], x_ci.at[:, pl.ds(mine, H), :], s, R_CI, partner))
        s_co = prepare(lambda j, s: copy(st_send.at[1], x_co.at[:, pl.ds(mine, H), :], s, R_CO, partner))
        s_yci = prepare(lambda j, s: copy(x_ci.at[j], yin.at[side, j], s, R_YIN + 4 * side + j, inner), C)
        s_ycip = prepare(lambda j, s: copy(x_ci.at[j], y_oth.at[j], s, R_YCI + j, partner), C)
        s_ye = prepare(lambda j, s: copy(ye, yein.at[side], s, R_YE + side, inner))
        s_yco = prepare(lambda j, s: copy(x_co.at[j], wco.at[side, j], s, R_YCO + 4 * side + j, inner), C)
        s_d = prepare(lambda j, s: copy(d_own.at[j], d_oth.at[j], s, R_DP + j, partner), C)
        s_p = prepare(lambda j, s: copy(p_own.at[j], yin.at[side, j], s, R_YIN + 4 * side + j, outer), C, has_outer)
        s_pp = prepare(lambda j, s: copy(p_own.at[j], p_oth.at[j], s, R_P + j, partner), C)
        s_q = prepare(lambda j, s: copy(qv, yein.at[side], s, R_YE + side, outer), 1, has_outer)
        s_r = prepare(lambda j, s: copy(r_own.at[j], r_oth.at[j], s, R_R + j, partner), C)

        def piece(ref, j):
            return ref.at[pl.ds(j * (N // K), N // K), :]

        s_in = prepare(lambda j, s: copy(piece(sin.at[0], j), piece(sin.at[side], j), s, R_S + K * side + j, inner), K, has_outer)
        s_sib = prepare(lambda j, s: copy(piece(sin.at[0], j), piece(sin.at[1], j), s, R_S + K + j, sibling), K, has_sibling)

        stack_rows(st_send.at[0], 0, tw.at[0], other, 0.2)
        s_ci()
        stack_rows(x_ci, mine, tw.at[0], mine, 0.2)
        split_rows(lhs.at[0], a_own, mine, True, 3)
        arrived(a_oth, R_A)
        split_rows(lhs.at[0], a_oth, other, True, 3)
        square(lhs.at[0], lhs.at[1])
        arrived(x_ci.at[:, pl.ds(other, H), :], R_CI)

        @pl.loop(0, C)
        def _(j):
            series(lhs, x_ci.at[j], x_ci.at[j], va, vb)
            s_yci(j)
            s_ycip(j)

        twist(1)
        stack_rows(st_send.at[1], 0, tw.at[1], other, 0.2)
        s_co()
        stack_rows(x_co, mine, tw.at[1], mine, 0.2)
        arrived(x_co.at[:, pl.ds(other, H), :], R_CO)

        @pl.loop(0, C)
        def _(j):
            series(lhs, x_co.at[j], x_co.at[j], va, vb)
            s_yco(j)

        arrived(es.at[pl.ds(other, H), :], R_E)
        ye[...] = 0.2 * es[...]
        series(lhs, ye, ye, va, vb)
        s_ye()
        split_chunks(lc.at[1], x_ci, mine, False, 2)
        for j in range(C):
            arrived(y_oth.at[j], R_YCI + j)
        split_chunks(lc.at[1], y_oth, other, False, 2)
        for j in range(C):
            arrived(d_own.at[j], R_D + j)
            s_d(j)
        split_chunks(lhs.at[0], d_own, mine, True, 3)
        for j in range(C):
            arrived(d_oth.at[j], R_DP + j)
        split_chunks(lhs.at[0], d_oth, other, True, 3)
        square(lhs.at[0], lhs.at[1])

        @pl.loop(0, C)
        def _(j):
            arrived(x_w.at[j], R_W + j)
            series(lhs, x_w.at[j], x_w.at[j], va, vb)
            put(p_own.at[j], lc.at[1], x_w.at[j], x_co.at[j])
            s_p(j)
            s_pp(j)

        arrived(zb, R_ZB)
        put(qv, lc.at[1], zb, ye, -1.0)
        s_q()
        split_chunks(lc.at[2], p_own, mine, False, 2)
        for j in range(C):
            arrived(p_oth.at[j], R_P + j)
        split_chunks(lc.at[2], p_oth, other, False, 2)

        def second(j):
            arrived(zwx.at[j], R_ZWX + j)
            put(r_own.at[j], lc.at[1], zwx.at[j])
            s_r(j)

        def relay(first, last):
            @pl.when(has_outer)
            def _():
                for j in range(first, last):
                    arrived(piece(sin.at[0], j), R_S + j)
                    s_in(j)
                    s_sib(j)

        pl.loop(0, C - 1)(second)
        relay(0, K // 2)
        second(C - 1)
        relay(K // 2, K)
        split_chunks(lc.at[0], r_own, mine, False, 2)
        res[...] = qv[...]

        @pl.when(has_outer)
        def _():
            put(res, lc.at[2], sin.at[0], res, -1.0)

        for j in range(C):
            arrived(r_oth.at[j], R_R + j)
        split_chunks(lc.at[0], r_oth, other, False, 2)

        @pl.when(has_second)
        def _():
            for j in range(K):
                arrived(piece(sin.at[1], j), R_S + K + j)
            put(res, lc.at[0], sin.at[1], res, -1.0, hand_over, 1 - r)

        finish()

    @pl.when(jnp.logical_not(odd))
    def _():
        is_c = role == 2
        sides = ((jnp.where(is_c, minus, plus), r), (jnp.where(is_c, plus, minus), r))
        prepare, finish = sender(2)
        prepare_c, finish_c = sender(24)
        prepare_a, finish_a = sender(24)

        def piece(ref, j):
            return ref.at[pl.ds(j * (N // K), N // K), :]

        s_t = prepare(lambda j, s: copy(tw.at[j], tw_oth.at[j], s, R_T + j, partner), 2)
        s_d = prepare(lambda j, s: copy(d_own.at[j], d_oth.at[j], s, R_DP + j, partner), C)
        s_dc = [prepare_c(lambda j, s, i=i: copy(d_own.at[j], d_own.at[j], s, R_D + j, sides[i]), C) for i in range(2)]
        s_w = [prepare_c(lambda j, s, i=i: copy(wco.at[i, j], x_w.at[j], s, R_W + j, sides[i]), C) for i in range(2)]
        s_zb = [prepare_c(lambda j, s, i=i: copy(zb, zb, s, R_ZB, sides[i])) for i in range(2)]
        def pair(ref, m):
            return ref.at[m % 2, m // 2]

        def opposite(m):
            return (jnp.where(m % 2 == 0, sides[1][0], sides[0][0]), r)

        s_zwp = prepare_c(lambda m, s: copy(pair(yin, m), pair(zwo, m), s, R_ZWP + m, partner), 2 * C)
        s_zwx = prepare_c(lambda m, s: copy(pair(yin, m), zwx.at[m // 2], s, R_ZWX + m // 2, opposite(m)), 2 * C)
        place = jnp.where(slab == 0, 1, 0)
        below = (jnp.where(slab == 0, slab_at(3), minus), r)
        s_sa = [
            prepare_a(lambda j, s: copy(piece(zb, j), piece(sin.at[0], j), s, R_S + j, sides[0]), K),
            prepare_a(lambda j, s: copy(piece(zb, j), piece(sin.at[place], j), s, R_S + K * place + j, below), K),
        ]

        twist(1)
        for i in range(2):
            s_t(i)
            split_rows(lc.at[i], tw.at[i], mine, False, 2)

        stack_rows(a_st, mine, a_own, mine, 1.0)
        arrived(a_oth, R_A)
        stack_rows(a_st, other, a_oth, mine, 1.0)
        for i in range(2):
            arrived(tw_oth.at[i], R_T + i)
            split_rows(lc.at[i], tw_oth.at[i], other, False, 2)
        arrived(es.at[pl.ds(other, H), :], R_E)

        @pl.loop(0, C)
        def _(j):
            arrived(yin.at[0, j], R_YIN + j)
            put(d_own.at[j], lc.at[0], yin.at[0, j], a_st.at[j], -1.0)

            @pl.when(has_minus)
            def _():
                arrived(yin.at[1, j], R_YIN + 4 + j)
                put(d_own.at[j], lc.at[1], yin.at[1, j], d_own.at[j], -1.0)

            @pl.when(is_c)
            def _():
                for i in range(2):
                    s_dc[i](j)

            s_d(j)

        split_chunks(lhs.at[0], d_own, mine, True, 3)
        for j in range(C):
            arrived(d_oth.at[j], R_DP + j)
        split_chunks(lhs.at[0], d_oth, other, True, 3)

        def couple(j):
            for i in range(2):
                arrived(wco.at[i, j], R_YCO + 4 * i + j)
                put(wco.at[i, j], lc.at[i], wco.at[i, j], scale=0.2)
                s_w[i](j)

        def inverted(m):
            series(lhs, pair(wco, m), pair(yin, m), va, vb)
            s_zwp(m)

        @pl.when(is_c)
        def _():
            couple(0)

        square(lhs.at[0], lhs.at[1])

        @pl.when(is_c)
        def _():
            @pl.loop(1, C)
            def _(j):
                couple(j)
                inverted(j - 1)

            s_zwx(0)
            s_zwx(1)

        for i in range(2):
            @pl.when(slab >= i)
            def _():
                arrived(yein.at[i], R_YE + i)
                put(es, lc.at[i], yein.at[i], es, -1.0)

        zb[...] = 0.2 * es[...]

        def send_tile(t):
            @pl.when(jnp.logical_not(is_c))
            def _():
                for j in range(t * K // 2, (t + 1) * K // 2):
                    for i in range(2):
                        s_sa[i](j)

        series(lhs, zb, zb, va, vb, send_tile)

        @pl.when(is_c)
        def _():
            for i in range(2):
                s_zb[i]()

            s_zwx(2)

            @pl.loop(C - 1, 2 * C)
            def _(m):
                inverted(m)
                s_zwx(m)

            for i in range(2):
                split_chunks(lc.at[i], yin.at[i], mine, False, 2)
            for i in range(2):
                for j in range(C):
                    arrived(zwo.at[i, j], R_ZWP + 2 * j + i)
                split_chunks(lc.at[i], zwo.at[i], other, False, 2)
            res[...] = zb[...]
            for i in range(2):
                @pl.when(slab < slabs - 1 - i)
                def _():
                    for j in range(K):
                        arrived(piece(sin.at[i], j), R_S + K * i + j)
                    put(res, lc.at[i], sin.at[i], res, 1.0, hand_over if i else None, 1 - r)

            finish_c()

        @pl.when(jnp.logical_not(is_c))
        def _():
            res[...] = zb[...]
            finish_a()

        finish()

    pl.when(jnp.logical_not(early))(c_f.start)
    own = res[pl.ds(mine, H), :]
    arrived(fin, R_FIN)
    oth = fin[...]
    re, im = unpack(jnp.where(r == 0, own, oth), jnp.where(r == 0, oth, own))
    o_ref[0] = re
    o_ref[1] = im
    c_f.wait_send()
    c_a.wait_send()
    c_e.wait_send()


def solution(mesh):
    slabs = mesh.shape["slab"]

    def body(diag_block, lower_block, upper_block, twist, excitation):
        vmem = pl.BlockSpec(memory_space=pltpu.VMEM)

        def f32(*shape):
            return pltpu.VMEM(shape, F32)

        rows, chunks, vector = f32(2, H, N), f32(C, N, Q), f32(N, Q)
        out = pl.pallas_call(
            functools.partial(kernel, slabs),
            out_shape=jax.ShapeDtypeStruct((2, H, Q), F32),
            in_specs=[pl.BlockSpec(memory_space=pl.ANY)] * 5,
            out_specs=vmem,
            scratch_shapes=[
                rows, f32(2, 2, H, N), f32(2, H, Q),
                pltpu.VMEM((1, N), jnp.int32),
                pltpu.VMEM((N, N), BF16),
                f32(2, 2, H, N), rows, f32(2, 2, H, N),
                chunks, f32(2, C, H, Q),
                chunks, chunks, chunks, chunks,
                f32(2, C, N, Q),
                chunks, chunks, chunks, chunks,
                chunks, chunks, chunks,
                f32(2, C, N, Q), f32(2, C, N, Q), f32(2, N, Q),
                vector, f32(H, Q),
                vector, vector, vector, vector, vector, vector,
                f32(2, N, Q), f32(H, Q),
                pltpu.VMEM((2, 3, 2, N, N), BF16),
                pltpu.VMEM((3, 2, 2, N, N), BF16),
                pltpu.SemaphoreType.DMA((N_SEND + 1,)),
                pltpu.SemaphoreType.DMA((N_RECV,)),
                pltpu.SemaphoreType.DMA((5,)),
            ],
            compiler_params=pltpu.CompilerParams(
                collective_id=0, has_side_effects=True, vmem_limit_bytes=60 * 1024 * 1024
            ),
        )(diag_block[0], lower_block[0], upper_block[0], twist, excitation[0])
        return out[None]

    spec = P("slab", None, "row", None)
    return jax.shard_map(
        body,
        mesh=mesh,
        in_specs=(spec, spec, spec, P("slab", None), spec),
        out_specs=spec,
        check_vma=False,
    )
```
